128 devices in a mesh: region: 8 (over x, core), blk: 16 (over y, z).
Axes of the slice: x: 4, y: 4, z: 4, core: 2. Of those that a mesh axis runs over, the one named last changes fastest.
Arguments:
- velocity: float32 [3, 128, 512, 256], P(None, 'region', 'blk'), may hold values from -5 to 5
- viscosity: float32 [128, 512, 256], P('region', 'blk'), may hold values from 0.02 to 0.1
- match_cell: int32 [131072], P(('region', 'blk')), may hold values from 0 to 131071
- wall_cell: int32 [131072], P(('region', 'blk')), may hold values from 0 to 131071
- match_dest: int32 [131072, 1], P(('region', 'blk')), may hold values from 0 to 127; in each aligned block of 1024 rows (0 to 1023, 1024 to 2047, ...) at most 16 rows name the same one
- match_count: int32 [128], P(('region', 'blk')), may hold values from 1 to 1024, 104857 in all
- wall_geom: float32 [4, 262144], P(None, ('region', 'blk')), may hold values from -1 to 1, as said below
Outputs:
- advanced: float32 [3, 128, 512, 256], P(None, 'region', 'blk')
- wall_log_stress: float32 [131072], P(('region', 'blk'))
The draws below stay inside these ranges and needn't reach their ends.
Inputs may be any that keep to these rules, and one draw needn't show every extreme that they name: `match_dest`: among the 1024 rows of one device at most 16 name the same owner, and some device reaches 16. The first match_count rows of a device's matching points are live; some device has all 1024 live. `match_cell`: local cell index of the device's 16 x 32 x 256 cells. `wall_cell`: local cell index of the device's 16 x 32 x 256 cells. `wall_geom`: row 0 lies in 0.02 to 0.3; rows 1 to 3 have magnitudes 0.3 to 1.
All inputs are finite; a program needn't handle non-finite values.
Results may differ from the reference program's by a relative error of at most 0.0003.
Values sent between devices are 32-bit elements; how exact they have to be, the bound alone decides.
No kernel may reach another device: no remote copies, remote signals or barrier semaphores. Data moves between devices by JAX's collectives and lax.ppermute only.
A program may use at most 192 MiB of HBM per device.

```python
import math
import jax
import jax.numpy as jnp
import numpy as np
from jax import lax

CX = 16
CY = 32
CZ = 256
MP_DEV = 1024
NEWTON = 2
NX = 128
NY = 512
CELLS_DEV = 131072
MATCH = 131072
CAP = 16
FACES = 262144
LIVE = 104857
N_REGION = 8
N_BLK = 16
DEVICES = 128


def draw_wall_geom(key, part):
    key_dist, key_size, key_sign = jax.random.split(key, 3)
    distance = jnp.exp(jax.random.uniform(key_dist, (1, FACES), jnp.float32, math.log(0.02), math.log(0.3)))
    magnitude = jax.random.uniform(key_size, (3, FACES), jnp.float32, 0.3, 1.0)
    signs = (jax.random.randint(key_sign, (3, FACES), 0, 2) * 2 - 1).astype(jnp.float32)
    return jnp.concatenate([distance, magnitude * signs], axis=0)


def with_ends(array, key, least, top_value):
    longest = array.shape.index(max(array.shape))
    spots = []
    for shift in (0, 1):
        where = [jax.random.randint(jax.random.fold_in(key, axis), (), 0, length) for axis, length in enumerate(array.shape)]
        where[longest] = (where[longest] + shift) % array.shape[longest]
        spots.append(tuple(where))
    return array.at[spots[0]].set(least).at[spots[1]].set(top_value)


def shard_levels(key, shape, shards, least, top_value):
    gain = 1.0
    for position, parts in shards:
        steps = jax.random.uniform(jax.random.fold_in(jax.random.fold_in(key, 6), position), (parts,), jnp.float32, least / len(shards), top_value / len(shards))
        gain = gain * jnp.repeat(jnp.exp(steps), shape[position] // parts).reshape((-1,) + (1,) * (len(shape) - 1 - position))
    return gain


def split_up(number_of, total, limit, slope):
    portions = [(1 << 20) // math.isqrt(standing ** slope) + 1 for standing in range(2, number_of + 1)]
    surplus, given = total - limit - (number_of - 1), [1] * (number_of - 1)
    while surplus > 0:
        movable = [i for i in range(number_of - 1) if given[i] < limit]
        whole, budget = sum([portions[i] for i in movable]), surplus
        for i in movable:
            extra = min(limit - given[i], max(1, budget * portions[i] // whole), surplus)
            given[i] = given[i] + extra
            surplus = surplus - extra
    return np.array([limit] + given)


def ragged_sizes(stream_key, amount, total, bound, slope):
    if amount == 2:
        one = jax.random.randint(stream_key, (), max(1, total - bound), min(bound, total - 1) + 1)
        return jnp.stack([one, total - one])
    lengths = jnp.asarray(split_up(amount, total, bound, slope), jnp.int32)
    couples = (amount - 1) // 2
    source_of, taker = lengths[1:1 + 2 * couples:2], lengths[2:2 + 2 * couples:2]
    room = jnp.minimum(source_of - 1, bound - taker)
    passed = jax.random.randint(jax.random.fold_in(stream_key, 1), (couples,), 0, 1 << 20) % (room + 1)
    lengths = lengths.at[1:1 + 2 * couples:2].set(source_of - passed).at[2:2 + 2 * couples:2].set(taker + passed)
    return lengths[jax.random.permutation(jax.random.fold_in(stream_key, 2), amount)]


def deal_out(own_key, own, number, rows, count, top, bound, lean):
    order = jax.random.permutation(own_key, count)
    heavy_load, usual = load_shares(count, rows * top, bound, lean, True), load_shares(count, rows * top, bound, lean, False)
    places = jnp.arange(count)

    def named(tallies, turn):
        used = int((tallies > 0).sum())
        fixed = max(1, used // 4)
        passed = fixed + (places - fixed + turn * (used - fixed)) % max(1, count - fixed)
        return jnp.zeros((count,), jnp.int32).at[order[jnp.where(places < fixed, places, passed)]].set(jnp.asarray(tallies, jnp.int32))

    tallies = jnp.where(number % 4 == 0, named(heavy_load, number // 4), named(usual, number - number // 4 - 1))
    mixed = jax.random.permutation(jax.random.fold_in(own, 3), count)
    donor, taker = mixed[0:count // 2 * 2:2], mixed[1:count // 2 * 2:2]
    slack = jnp.minimum(tallies[donor] - 1, bound - tallies[taker]) // 2
    slack = jnp.where((donor == order[0]) | (taker == order[0]) | (tallies[taker] == 0), 0, jnp.maximum(slack, 0))
    passed = jax.random.randint(jax.random.fold_in(own, 4), (count // 2,), 0, 1 << 20) % (slack + 1)
    tallies = tallies.at[donor].add(-passed).at[taker].add(passed)
    labels = jnp.searchsorted(jnp.cumsum(tallies), jnp.arange(rows * top), side="right").astype(jnp.int32)
    grid = labels.reshape(top, rows).T
    grid = grid[jax.random.permutation(jax.random.fold_in(own, 1), rows)]
    turn = jax.random.randint(jax.random.fold_in(own, 2), (rows, 1), 0, top)
    return jnp.take_along_axis(grid, (jnp.arange(top)[None, :] + turn) % top, axis=1)


def load_shares(count, total, bound, slope, full):
    weights = [(1 << 20) // math.isqrt(grade ** slope) + 1 for grade in range(1, count + 1)]
    largest = bound if full else min(bound, max(-(-total // count), total * weights[0] // sum(weights)))
    least = 1 if total - largest >= count - 1 else 0
    given, surplus = [largest] + [least] * (count - 1), total - largest - least * (count - 1)
    while surplus > 0:
        candidates = [i for i in range(1, count) if given[i] < largest] or [i for i in range(1, count) if given[i] < bound]
        mass, remaining = sum([weights[i] for i in candidates]), surplus
        for i in candidates:
            addition = min(bound - given[i], max(1, remaining * weights[i] // mass), surplus)
            given[i] = given[i] + addition
            surplus = surplus - addition
    return np.array(given)


def bell_draw(key, dims, scale, bound, cuts=(), kind=jnp.bfloat16):
    values = scale * jax.random.normal(key, dims, jnp.float32)
    if cuts:
        values = values * shard_levels(key, dims, cuts, -0.22, 0.18)
    return jnp.clip(values, -bound, bound).astype(kind)


def setup_inputs(seed: int = 0) -> dict:
    keys = jax.random.split(jax.random.key(seed), 8)
    velocity = bell_draw(keys[0], (3, NX, NY, CZ), 1.0, 5.0, ((1, 8), (2, 16)), jnp.float32)
    viscosity = jnp.clip(jnp.exp(math.log(0.1) - 1.609438 * jax.random.uniform(keys[1], (NX, NY, CZ), jnp.float32) ** shard_levels(keys[1], (NX, NY, CZ), ((0, 8), (1, 16)), -0.2, 0.2)), 0.02, 0.1)
    match_cell = with_ends(jax.random.randint(keys[2], (MATCH,), 0, CELLS_DEV), jax.random.fold_in(keys[2], 1), 0, CELLS_DEV - 1).astype(jnp.int32)
    wall_cell = with_ends(jax.random.randint(keys[3], (MATCH,), 0, CELLS_DEV), jax.random.fold_in(keys[3], 1), 0, CELLS_DEV - 1).astype(jnp.int32)
    match_dest_keys = jax.random.split(jax.random.fold_in(keys[4], 1), MATCH // MP_DEV)
    match_dest_turns = jax.random.permutation(jax.random.fold_in(keys[4], 3), MATCH // MP_DEV)
    match_dest = jax.vmap(lambda own, number: deal_out(jax.random.fold_in(keys[4], 2), own, number, MP_DEV, DEVICES, 1, CAP, 2))(match_dest_keys, match_dest_turns).reshape((MATCH, 1))
    match_count = ragged_sizes(keys[5], DEVICES, LIVE, MP_DEV, 2).astype(jnp.int32)
    wall_geom = draw_wall_geom(jax.random.fold_in(keys[7], 71), 0)
    return dict(velocity=velocity, viscosity=viscosity, match_cell=match_cell, wall_cell=wall_cell, match_dest=match_dest, match_count=match_count, wall_geom=wall_geom)


KAPPA = 0.41
DAMPING = 26.0
NU_WALL = 0.0002
WALL_DY = 0.0005
TIME_STEP = 0.1
SPEED_FLOOR = 0.5
GUESS_RATIO = 14.0

def profile_table():
    fraction = jnp.arange(32, dtype=jnp.float32) / 31.0
    heights = fraction * fraction
    upper_end = jnp.concatenate([heights[1:], heights[-1:]])
    lower_end = jnp.concatenate([heights[:1], heights[:-1]])
    return (heights, 0.5 * (upper_end - lower_end))

def log_integral(log_speed, distance):
    heights, weights = profile_table()
    speed_now = jnp.exp(log_speed)[None, :]
    height = heights[:, None] * distance[None, :]
    van_driest = 1.0 - jnp.exp(-height * speed_now / (NU_WALL * DAMPING))
    eddy_visc = KAPPA * height * speed_now * van_driest * van_driest
    integrand = weights[:, None] * distance[None, :] * speed_now * speed_now / (NU_WALL + eddy_visc)
    return jnp.log(lax.optimization_barrier(jnp.sum(integrand, axis=0)))

def wall_solve(samples, geometry):
    distance = geometry[0]
    normal = geometry[1:4]
    normal = normal / jnp.sqrt(lax.optimization_barrier(jnp.sum(normal * normal, axis=0)))[None]
    normal_part = lax.optimization_barrier(jnp.sum(samples * normal, axis=0))
    tangent = samples - normal_part[None] * normal
    tangent_speed = jnp.maximum(jnp.sqrt(lax.optimization_barrier(jnp.sum(tangent * tangent, axis=0))), SPEED_FLOOR)
    target = jnp.log(tangent_speed)
    log_speed = target - jnp.log(GUESS_RATIO)
    slope_of = jax.grad(lambda values: jnp.sum(log_integral(values, distance)))
    for newton_step in range(NEWTON):
        log_speed = log_speed - (log_integral(log_speed, distance) - target) / slope_of(log_speed)
    stress = jnp.exp(2.0 * log_speed)
    return jnp.concatenate([(-stress / tangent_speed)[None] * tangent, (2.0 * log_speed)[None]], axis=0)

def tendency(padded, section_field, viscosity, forcing):
    extent = section_field.shape

    def window(axis_dim, offset):
        starts = [0, 2, 2, 2]
        starts[axis_dim] = starts[axis_dim] + offset
        limits = [starts[index] + extent[index] for index in range(4)]
        return lax.slice(padded, starts, limits)
    advect = jnp.zeros_like(section_field)
    spread = jnp.zeros_like(section_field)
    for axis_dim in (1, 2, 3):
        ahead_one = window(axis_dim, 1)
        behind_one = window(axis_dim, -1)
        ahead_two = window(axis_dim, 2)
        behind_two = window(axis_dim, -2)
        gradient = (8.0 * (ahead_one - behind_one) - (ahead_two - behind_two)) / 12.0
        advect = advect + section_field[axis_dim - 1][None] * gradient
        spread = spread + (16.0 * (ahead_one + behind_one) - (ahead_two + behind_two) - 30.0 * section_field) / 12.0
    return viscosity[None] * spread - advect + forcing

def reference(velocity, viscosity, match_cell, wall_cell, match_dest, match_count, wall_geom):
    devices = N_REGION * N_BLK
    slot_count = devices * CAP
    targets = match_dest[:, 0].reshape(devices, MP_DEV)
    is_live = jnp.arange(MP_DEV, dtype=jnp.int32)[None, :] < match_count[:, None]

    def ranks_of(pair):
        owner_row, live_row = pair
        owners = (owner_row[:, None] == jnp.arange(devices, dtype=jnp.int32)[None, :]) & live_row[:, None]
        running = jnp.cumsum(owners.astype(jnp.int32), axis=0) - 1
        return lax.optimization_barrier(jnp.sum(jnp.where(owners, running, 0), axis=1)).astype(jnp.int32)
    bucket_rank = lax.map(ranks_of, (targets, is_live))
    source = jnp.arange(devices, dtype=jnp.int32)[:, None]
    face_index = jnp.where(is_live, targets * slot_count + source * CAP + bucket_rank, 0).reshape(-1)
    geometry = jnp.take(wall_geom, face_index, axis=1)
    region_of = source // N_BLK
    block_of = source % N_BLK

    def global_index(local_cells):
        local_cells = local_cells.reshape(devices, MP_DEV)
        first_ix = local_cells // (CY * CZ)
        second_ix = local_cells // CZ % CY
        third_ix = local_cells % CZ
        return (((region_of * CX + first_ix) * NY + block_of * CY + second_ix) * CZ + third_ix).reshape(-1)
    match_global = global_index(match_cell)
    wall_global = global_index(wall_cell)
    live_flat = is_live.reshape(-1)

    def section_terms(section_field):
        flat_field = section_field.reshape(3, -1)
        samples = jnp.take(flat_field, match_global, axis=1)
        solved = wall_solve(samples, geometry)
        stress = jnp.where(live_flat[None], solved[:3], 0.0)
        forcing = jnp.zeros_like(flat_field).at[:, wall_global].add(stress / WALL_DY)
        log_stress = jnp.where(live_flat, solved[3], 0.0)
        padded = jnp.pad(section_field, ((0, 0), (2, 2), (2, 2), (2, 2)))
        return (tendency(padded, section_field, viscosity, forcing.reshape(section_field.shape)), log_stress)
    rate_first, first_stress = section_terms(velocity)
    first = velocity + TIME_STEP * rate_first
    rate_second, log_stress = section_terms(first)
    advanced = 0.5 * velocity + 0.5 * (first + TIME_STEP * rate_second)
    return (advanced, log_stress)
```

```python
import jax
import jax.numpy as jnp
from jax import lax
from jax.experimental import pallas as pl
from jax.experimental.pallas import tpu as pltpu
from jax.sharding import PartitionSpec as P

NEWTON = 2

KAPPA = 0.41
DAMPING = 26.0
NU_WALL = 0.0002
WALL_DY = 0.0005
TIME_STEP = 0.1
SPEED_FLOOR = 0.5
GUESS_RATIO = 14.0
ETAS = 32
PIECES = 3
F32 = jnp.float32
BF16 = jnp.bfloat16


def pieces_of(values, count):
    parts = []
    rest = values
    for index in range(count):
        part = rest.astype(BF16)
        parts.append(part)
        if index + 1 < count:
            rest = rest - part.astype(F32)
    return parts


def as_row(block):
    rows = block.shape[0]
    return jnp.concatenate([block[i : i + 1, :] for i in range(rows)], axis=1)


def row_iota(shape):
    return lax.broadcasted_iota(jnp.int32, shape, 0)


def fill_padded(padded, field_ref, xlo_ref, xhi_ref, ylo_ref, yhi_ref):
    comps, nx, ny, nz = field_ref.shape
    region = lax.axis_index("region")
    block = lax.axis_index("blk")
    no_xlo = region == 0
    no_xhi = region == lax.axis_size("region") - 1
    no_ylo = block == 0
    no_yhi = block == lax.axis_size("blk") - 1
    for c in range(comps):
        padded[c, 2 : 2 + nx, 8 : 8 + ny, :] = field_ref[c]
        padded[c, 0:2, 8 : 8 + ny, :] = jnp.where(no_xlo, 0.0, xlo_ref[c])
        padded[c, 2 + nx : 4 + nx, 8 : 8 + ny, :] = jnp.where(no_xhi, 0.0, xhi_ref[c])
        padded[c, 2 : 2 + nx, 6:8, :] = jnp.where(no_ylo, 0.0, ylo_ref[c])
        padded[c, 2 : 2 + nx, 8 + ny : 10 + ny, :] = jnp.where(no_yhi, 0.0, yhi_ref[c])


def stencil(padded, viscosity_ref, emit):
    comps = padded.shape[0]
    nx, ny, nz = viscosity_ref.shape
    lane = lax.broadcasted_iota(jnp.int32, (8, nz), 1)

    def plane(x, carry):
        for tile in range(ny // 8):
            y = 8 + 8 * tile
            centers = [padded[c, x + 2, y : y + 8, :] for c in range(comps)]
            scaled = [value * (1.0 / 12.0) for value in centers]
            visc = viscosity_ref[x, 8 * tile : 8 * tile + 8, :] * (1.0 / 12.0)
            for c in range(comps):
                here = centers[c]
                near = None
                for axis in range(3):
                    if axis == 0:
                        a1 = padded[c, x + 3, y : y + 8, :]
                        b1 = padded[c, x + 1, y : y + 8, :]
                        a2 = padded[c, x + 4, y : y + 8, :]
                        b2 = padded[c, x, y : y + 8, :]
                    elif axis == 1:
                        a1 = padded[c, x + 2, y + 1 : y + 9, :]
                        b1 = padded[c, x + 2, y - 1 : y + 7, :]
                        a2 = padded[c, x + 2, y + 2 : y + 10, :]
                        b2 = padded[c, x + 2, y - 2 : y + 6, :]
                    else:
                        a1 = jnp.where(lane < nz - 1, pltpu.roll(here, nz - 1, 1), 0.0)
                        b1 = jnp.where(lane >= 1, pltpu.roll(here, 1, 1), 0.0)
                        a2 = jnp.where(lane < nz - 2, pltpu.roll(here, nz - 2, 1), 0.0)
                        b2 = jnp.where(lane >= 2, pltpu.roll(here, 2, 1), 0.0)
                    slope = 8.0 * (a1 - b1) - (a2 - b2)
                    if near is None:
                        near = a1 + b1
                        far = a2 + b2
                        advect = scaled[axis] * slope
                    else:
                        near = near + (a1 + b1)
                        far = far + (a2 + b2)
                        advect = advect + scaled[axis] * slope
                spread = 16.0 * near - far - 90.0 * here
                emit(c, x, 8 * tile, here, visc * spread - advect)
        return carry

    lax.fori_loop(0, nx, plane, 0)


def sample_at(field_ref, cells, split, picked):
    comps, nx, ny, nz = field_ref.shape
    points = cells.shape[1]
    rows = nx * ny
    for c in range(comps):
        values = field_ref[c].reshape(rows, nz)
        for index, part in enumerate(pieces_of(values, PIECES)):
            split[c * rows : (c + 1) * rows, index * nz : (index + 1) * nz] = part
    lane_cell = cells & (nz - 1)
    row_cell = cells // nz
    width = 256
    sums = [[] for _ in range(comps)]
    for start in range(0, points, width):
        lanes = slice(start, start + width)
        hot = jnp.where(row_iota((nz, width)) == lane_cell[:, lanes], 1.0, 0.0).astype(BF16)
        hots = jnp.concatenate([hot] * PIECES, axis=0)
        picked[...] = jnp.dot(split[...], hots, preferred_element_type=F32)
        mask = row_iota((rows, width)) == row_cell[:, lanes]
        for c in range(comps):
            block = picked[c * rows : (c + 1) * rows, :]
            sums[c].append(jnp.sum(jnp.where(mask, block, 0.0), axis=0, keepdims=True))
    return [jnp.concatenate(parts, axis=1) for parts in sums]


def scatter_sum(stresses, cells, live, shape):
    comps, nx, ny, nz = shape
    points = cells.shape[1]
    rows = nx * ny
    lane_cell = cells & (nz - 1)
    row_cell = cells // nz
    hot = jnp.where(row_iota((rows, points)) == row_cell, 1.0, 0.0).astype(BF16)
    match = (row_iota((nz, points)) == lane_cell) & live
    total = None
    split = [pieces_of(value, PIECES) for value in stresses]
    for index in range(PIECES):
        spread = jnp.concatenate(
            [
                jnp.where(match, split[c][index].astype(F32), 0.0).astype(BF16)
                for c in range(comps)
            ],
            axis=0,
        )
        part = lax.dot_general(
            hot, spread, (((1,), (1,)), ((), ())), preferred_element_type=F32
        )
        total = part if total is None else total + part
    return total


def wall_solve(samples, distance, normals):
    points = distance.shape[1]
    normal_part = sum(s * n for s, n in zip(samples, normals))
    tangent = [s - normal_part * n for s, n in zip(samples, normals)]
    speed = jnp.maximum(jnp.sqrt(sum(t * t for t in tangent)), SPEED_FLOOR)
    target = jnp.log(speed)
    log_speed = target - jnp.log(jnp.full_like(target, GUESS_RATIO))
    index = row_iota((ETAS, points)).astype(F32)
    top = ETAS - 1.0
    eta = (index / top) * (index / top)
    upper = jnp.minimum(index + 1.0, top) / top
    lower = jnp.maximum(index - 1.0, 0.0) / top
    weight = 0.5 * (upper * upper - lower * lower)
    for _ in range(NEWTON):
        pace = jnp.exp(log_speed)
        height = eta * (distance * pace)
        decay = height * (1.0 / (NU_WALL * DAMPING))
        fade = jnp.exp(-decay)
        damp = 1.0 - fade
        mixing = KAPPA * height * damp
        share = weight / (NU_WALL + mixing * damp)
        growth = mixing * (damp + 2.0 * decay * fade)
        total = jnp.sum(share, axis=0, keepdims=True)
        change = jnp.sum(share * growth / (NU_WALL + mixing * damp), axis=0, keepdims=True)
        value = jnp.log(distance * pace * pace * total) - target
        log_speed = log_speed - value / (2.0 - change / total)
    stress = jnp.exp(2.0 * log_speed)
    factor = -stress / speed
    return [factor * t for t in tangent], 2.0 * log_speed


def first_kernel(
    velocity_ref, viscosity_ref, xlo_ref, xhi_ref, ylo_ref, yhi_ref, match_ref, dest_ref,
    base_ref, samples_ref, rank_ref, padded, split, picked,
):
    points = match_ref.shape[0] * match_ref.shape[1]
    cells = as_row(match_ref[...])
    samples = sample_at(velocity_ref, cells, split, picked)
    for c in range(3):
        samples_ref[c : c + 1, :] = samples[c]
    owners = as_row(dest_ref[...])
    devices = lax.axis_size("region") * lax.axis_size("blk")
    width = 128
    before = jnp.where(
        row_iota((width, width)) < lax.broadcasted_iota(jnp.int32, (width, width), 1), 1.0, 0.0
    )
    table = jnp.concatenate([before, jnp.ones((width, width), F32)], axis=0).astype(BF16)
    earlier = jnp.zeros((devices, width), F32)
    for start in range(0, points, width):
        hot = jnp.where(row_iota((devices, width)) == owners[:, start : start + width], 1.0, 0.0)
        both = jnp.concatenate([hot, earlier], axis=1).astype(BF16)
        running = jnp.dot(both, table, preferred_element_type=F32)
        rank_ref[0:1, start : start + width] = jnp.sum(hot * running, axis=0, keepdims=True)
        earlier = earlier + hot
    fill_padded(padded, velocity_ref, xlo_ref, xhi_ref, ylo_ref, yhi_ref)

    def emit(c, x, y, here, rate):
        base_ref[c, x, y : y + 8, :] = here + TIME_STEP * rate

    stencil(padded, viscosity_ref, emit)


def live_row(count_ref, points):
    return lax.broadcasted_iota(jnp.int32, (1, points), 1) < count_ref[0]


def stress_kernel(
    count_ref, arrived_ref, dest_ref, wall_ref, rank_ref, samples_ref, base_ref,
    first_ref, xlow_ref, xhigh_ref, ylow_ref, yhigh_ref, geometry_ref,
):
    comps, nx, ny, nz = base_ref.shape
    devices, fields = arrived_ref.shape
    capacity = fields // 4
    points = wall_ref.shape[0] * wall_ref.shape[1]
    owners = as_row(dest_ref[...])
    hot = jnp.where(row_iota((devices, points)) == owners, 1.0, 0.0).astype(BF16)
    table = None
    for part in pieces_of(arrived_ref[...], 3):
        term = lax.dot_general(
            part, hot, (((0,), (0,)), ((), ())), preferred_element_type=F32
        )
        table = term if table is None else table + term
    rank = rank_ref[0:1, :].astype(jnp.int32)
    mask = row_iota((capacity, points)) == rank
    rows = [
        jnp.sum(
            jnp.where(mask, table[k * capacity : (k + 1) * capacity, :], 0.0),
            axis=0, keepdims=True,
        )
        for k in range(4)
    ]
    distance = rows[0]
    length = jnp.sqrt(rows[1] * rows[1] + rows[2] * rows[2] + rows[3] * rows[3])
    normals = [row / length for row in rows[1:]]
    geometry_ref[0:1, :] = distance
    for k in range(3):
        geometry_ref[k + 1 : k + 2, :] = normals[k]
    samples = [samples_ref[c : c + 1, :] for c in range(3)]
    stress, _ = wall_solve(samples, distance, normals)
    live = live_row(count_ref, points)
    stress = [jnp.where(live, value, 0.0) for value in stress]
    force = scatter_sum(stress, as_row(wall_ref[...]), live, base_ref.shape)
    for c in range(comps):
        block = force[:, c * nz : (c + 1) * nz] * (TIME_STEP / WALL_DY)
        first_ref[c] = base_ref[c] + block.reshape(nx, ny, nz)
        xlow_ref[c] = first_ref[c, 0:2]
        xhigh_ref[c] = first_ref[c, nx - 2 : nx]
        ylow_ref[c] = first_ref[c, :, 0:2, :]
        yhigh_ref[c] = first_ref[c, :, ny - 2 : ny, :]


def second_kernel(
    count_ref, first_ref, match_ref, wall_ref, geometry_ref, force_ref, log_ref, split, picked,
):
    comps, nx, ny, nz = first_ref.shape
    points = wall_ref.shape[0] * wall_ref.shape[1]
    samples = sample_at(first_ref, as_row(match_ref[...]), split, picked)
    distance = geometry_ref[0:1, :]
    normals = [geometry_ref[k : k + 1, :] for k in range(1, 4)]
    stress, log_stress = wall_solve(samples, distance, normals)
    live = live_row(count_ref, points)
    log_stress = jnp.where(live, log_stress, 0.0)
    for i in range(log_ref.shape[0]):
        log_ref[i : i + 1, :] = log_stress[:, i * 128 : (i + 1) * 128]
    stress = [jnp.where(live, value, 0.0) for value in stress]
    force = scatter_sum(stress, as_row(wall_ref[...]), live, first_ref.shape)
    for c in range(comps):
        block = force[:, c * nz : (c + 1) * nz] * (0.5 * TIME_STEP / WALL_DY)
        force_ref[c] = block.reshape(nx, ny, nz)


def last_kernel(
    velocity_ref, viscosity_ref, first_ref, force_ref, xlo_ref, xhi_ref, ylo_ref, yhi_ref,
    advanced_ref, padded,
):
    fill_padded(padded, first_ref, xlo_ref, xhi_ref, ylo_ref, yhi_ref)

    def emit(c, x, y, here, rate):
        rows = slice(y, y + 8)
        mean = 0.5 * (velocity_ref[c, x, rows, :] + here)
        advanced_ref[c, x, rows, :] = mean + (
            0.5 * TIME_STEP * rate + force_ref[c, x, rows, :]
        )

    stencil(padded, viscosity_ref, emit)


def ring(axis, step):
    count = lax.axis_size(axis)
    return [(i, (i + step) % count) for i in range(count)]


def shift(block, axis, step):
    return lax.ppermute(block, axis, ring(axis, step))


def exchange(xlow, xhigh, ylow, yhigh):
    return (
        shift(xhigh, "region", 1),
        shift(xlow, "region", -1),
        shift(yhigh, "blk", 1),
        shift(ylow, "blk", -1),
    )


def local(velocity, viscosity, match_cell, wall_cell, match_dest, match_count, wall_geom):
    devices = lax.axis_size("region") * lax.axis_size("blk")
    capacity = wall_geom.shape[1] // devices
    points = match_cell.shape[0]
    comps, nx, ny, nz = velocity.shape
    field = jax.ShapeDtypeStruct(velocity.shape, F32)
    xface = jax.ShapeDtypeStruct((comps, 2, ny, nz), F32)
    yface = jax.ShapeDtypeStruct((comps, nx, 2, nz), F32)
    rowed = jax.ShapeDtypeStruct((4, points), F32)
    square = (points // 128, 128)
    match = match_cell.reshape(square)
    wall = wall_cell.reshape(square)
    dest = match_dest.reshape(square)
    vmem = pl.BlockSpec(memory_space=pltpu.VMEM)
    smem = pl.BlockSpec(memory_space=pltpu.SMEM)
    padded = pltpu.VMEM((comps, nx + 4, ny + 16, nz), F32)
    split = pltpu.VMEM((comps * nx * ny, PIECES * nz), BF16)
    picked = pltpu.VMEM((comps * nx * ny, 256), F32)

    outgoing = wall_geom.reshape(4, devices, capacity).transpose(1, 0, 2).reshape(devices, -1)
    arrived = lax.all_to_all(
        outgoing, ("region", "blk"), split_axis=0, concat_axis=0, tiled=True
    )
    halos = exchange(
        velocity[:, 0:2], velocity[:, nx - 2 :], velocity[:, :, 0:2], velocity[:, :, ny - 2 :]
    )
    base, samples, rank = pl.pallas_call(
        first_kernel,
        out_shape=(field, rowed, jax.ShapeDtypeStruct((1, points), F32)),
        in_specs=[vmem] * 8,
        out_specs=(vmem,) * 3,
        scratch_shapes=[padded, split, picked],
        name="first",
    )(velocity, viscosity, *halos, match, dest)
    first, *faces, geometry = pl.pallas_call(
        stress_kernel,
        out_shape=(field, xface, xface, yface, yface, rowed),
        in_specs=[smem] + [vmem] * 6,
        out_specs=(vmem,) * 6,
        name="stress",
    )(match_count, arrived, dest, wall, rank, samples, base)
    halos = exchange(*faces)
    force, log_stress = pl.pallas_call(
        second_kernel,
        out_shape=(field, jax.ShapeDtypeStruct(square, F32)),
        in_specs=[smem] + [vmem] * 4,
        out_specs=(vmem,) * 2,
        scratch_shapes=[split, picked],
        name="second",
    )(match_count, first, match, wall, geometry)
    advanced = pl.pallas_call(
        last_kernel,
        out_shape=field,
        in_specs=[vmem] * 8,
        out_specs=vmem,
        scratch_shapes=[padded],
        name="last",
    )(velocity, viscosity, first, force, *halos)
    return (advanced, log_stress.reshape(points))


def solution(mesh):
    placed = (
        P(None, "region", "blk", None),
        P("region", "blk", None),
        P(("region", "blk")),
        P(("region", "blk")),
        P(("region", "blk"), None),
        P(("region", "blk")),
        P(None, ("region", "blk")),
    )
    return jax.shard_map(
        local,
        mesh=mesh,
        in_specs=placed,
        out_specs=(P(None, "region", "blk", None), P(("region", "blk"))),
        check_vma=False,
    )
```

```python
import jax
import jax.numpy as jnp
from jax import lax
from jax.experimental import pallas as pl
from jax.experimental.pallas import tpu as pltpu
from jax.sharding import PartitionSpec as P

NEWTON = 2

KAPPA = 0.41
DAMPING = 26.0
NU_WALL = 0.0002
WALL_DY = 0.0005
TIME_STEP = 0.1
SPEED_FLOOR = 0.5
GUESS_RATIO = 14.0
ETAS = 32
PIECES = 2
F32 = jnp.float32
BF16 = jnp.bfloat16


def pieces_of(values, count):
    parts = []
    rest = values
    for index in range(count):
        part = rest.astype(BF16)
        parts.append(part)
        if index + 1 < count:
            rest = rest - part.astype(F32)
    return parts


def as_row(block):
    rows = block.shape[0]
    return jnp.concatenate([block[i : i + 1, :] for i in range(rows)], axis=1)


def row_iota(shape):
    return lax.broadcasted_iota(jnp.int32, shape, 0)


def even_side(axis):
    return lax.axis_index(axis) % 2 == 0


def at_end(axis):
    place = lax.axis_index(axis)
    return (place == 0) | (place == lax.axis_size(axis) - 1)


def fill_padded(padded, field_ref, xa_ref, xb_ref, ya_ref, yb_ref):
    comps, nx, ny, nz = field_ref.shape
    even_x, even_y = even_side("region"), even_side("blk")
    end_x, end_y = at_end("region"), at_end("blk")
    spot_a = jnp.where(even_x, nx + 2, 0)
    spot_b = nx + 2 - spot_a
    for c in range(comps):
        near_x = xa_ref[c]
        far_x = jnp.where(end_x, 0.0, xb_ref[c])
        near_y = ya_ref[c]
        far_y = jnp.where(end_y, 0.0, yb_ref[c])
        low_y = jnp.where(even_y, far_y, near_y)
        high_y = jnp.where(even_y, near_y, far_y)
        for h in range(nz // 128):
            lanes = slice(128 * h, 128 * h + 128)
            padded[c, h, 2 : 2 + nx, 8 : 8 + ny, :] = field_ref[c, :, :, lanes]
            padded[c, h, pl.ds(spot_a, 2), 8 : 8 + ny, :] = near_x[:, :, lanes]
            padded[c, h, pl.ds(spot_b, 2), 8 : 8 + ny, :] = far_x[:, :, lanes]
            padded[c, h, 2 : 2 + nx, 6:8, :] = low_y[:, :, lanes]
            padded[c, h, 2 : 2 + nx, 8 + ny : 10 + ny, :] = high_y[:, :, lanes]


def stencil(padded, viscosity_ref, step, emit):
    comps, halves = padded.shape[:2]
    nx, ny, _ = viscosity_ref.shape
    lane = lax.broadcasted_iota(jnp.int32, (8, 128), 1)
    top = [lane < 127, lane < 126]
    bottom = [lane >= 1, lane >= 2]
    scale = step / 12.0

    def plane(x, carry):
        for tile in range(ny // 8):
            y = 8 + 8 * tile
            here = [
                [padded[c, h, x + 2, y : y + 8, :] for h in range(halves)] for c in range(comps)
            ]
            for h in range(halves):
                lanes = slice(128 * h, 128 * h + 128)
                visc = viscosity_ref[x, 8 * tile : 8 * tile + 8, lanes] * scale
                speed = [here[c][h] * scale for c in range(comps)]
                for c in range(comps):

                    def along_z(shift):
                        count = abs(shift)
                        rolled = pltpu.roll(here[c][h], (-shift) % 128, 1)
                        other = h + (1 if shift > 0 else -1)
                        if 0 <= other < halves:
                            rest = pltpu.roll(here[c][other], (-shift) % 128, 1)
                        else:
                            rest = 0.0
                        inside = top[count - 1] if shift > 0 else bottom[count - 1]
                        return jnp.where(inside, rolled, rest)

                    def at(axis, shift):
                        if axis == 0:
                            return padded[c, h, x + 2 + shift, y : y + 8, :]
                        if axis == 1:
                            return padded[c, h, x + 2, y + shift : y + shift + 8, :]
                        return along_z(shift)

                    for axis in range(3):
                        a1, b1, a2, b2 = (at(axis, shift) for shift in (1, -1, 2, -2))
                        slope = 8.0 * (a1 - b1) - (a2 - b2)
                        if axis == 0:
                            near, far = a1 + b1, a2 + b2
                            advect = speed[axis] * slope
                        else:
                            near, far = near + (a1 + b1), far + (a2 + b2)
                            advect = advect + speed[axis] * slope
                    spread = 16.0 * near - far - 90.0 * here[c][h]
                    rows = slice(8 * tile, 8 * tile + 8)
                    emit((c, x, rows, lanes), here[c][h], visc * spread - advect)
        return carry

    lax.fori_loop(0, nx, plane, 0)


def sample_at(field_ref, cells, split, picked):
    comps, nx, ny, nz = field_ref.shape
    points = cells.shape[1]
    rows = nx * ny
    for c in range(comps):
        values = field_ref[c].reshape(rows, nz)
        for index, part in enumerate(pieces_of(values, PIECES)):
            split[c * rows : (c + 1) * rows, index * nz : (index + 1) * nz] = part
    lane_cell = cells & (nz - 1)
    row_cell = cells // nz
    width = 256
    sums = [[] for _ in range(comps)]
    for start in range(0, points, width):
        lanes = slice(start, start + width)
        hot = jnp.where(row_iota((nz, width)) == lane_cell[:, lanes], 1.0, 0.0).astype(BF16)
        hots = jnp.concatenate([hot] * PIECES, axis=0)
        picked[...] = jnp.dot(split[...], hots, preferred_element_type=F32)
        mask = row_iota((rows, width)) == row_cell[:, lanes]
        for c in range(comps):
            block = picked[c * rows : (c + 1) * rows, :]
            sums[c].append(jnp.sum(jnp.where(mask, block, 0.0), axis=0, keepdims=True))
    return [jnp.concatenate(parts, axis=1) for parts in sums]


def scatter_sum(stresses, cells, live, shape):
    comps, nx, ny, nz = shape
    points = cells.shape[1]
    rows = nx * ny
    lane_cell = cells & (nz - 1)
    row_cell = cells // nz
    hot = jnp.where(row_iota((rows, points)) == row_cell, 1.0, 0.0).astype(BF16)
    match = (row_iota((nz, points)) == lane_cell) & live
    total = None
    split = [pieces_of(value, PIECES) for value in stresses]
    for index in range(PIECES):
        spread = jnp.concatenate(
            [
                jnp.where(match, split[c][index].astype(F32), 0.0).astype(BF16)
                for c in range(comps)
            ],
            axis=0,
        )
        part = lax.dot_general(
            hot, spread, (((1,), (1,)), ((), ())), preferred_element_type=F32
        )
        total = part if total is None else total + part
    return total


def wall_solve(samples, distance, normals):
    points = distance.shape[1]
    normal_part = sum(s * n for s, n in zip(samples, normals))
    tangent = [s - normal_part * n for s, n in zip(samples, normals)]
    speed = jnp.maximum(jnp.sqrt(sum(t * t for t in tangent)), SPEED_FLOOR)
    target = jnp.log(speed)
    log_speed = target - jnp.log(jnp.full_like(target, GUESS_RATIO))
    index = row_iota((ETAS, points)).astype(F32)
    top = ETAS - 1.0
    eta = (index / top) * (index / top)
    upper = jnp.minimum(index + 1.0, top) / top
    lower = jnp.maximum(index - 1.0, 0.0) / top
    weight = 0.5 * (upper * upper - lower * lower)
    for _ in range(NEWTON):
        pace = jnp.exp(log_speed)
        height = eta * (distance * pace)
        decay = height * (1.0 / (NU_WALL * DAMPING))
        fade = jnp.exp(-decay)
        damp = 1.0 - fade
        mixing = KAPPA * height * damp
        share = weight / (NU_WALL + mixing * damp)
        growth = mixing * (damp + 2.0 * decay * fade)
        total = jnp.sum(share, axis=0, keepdims=True)
        change = jnp.sum(share * growth / (NU_WALL + mixing * damp), axis=0, keepdims=True)
        value = jnp.log(distance * pace * pace * total) - target
        log_speed = log_speed - value / (2.0 - change / total)
    stress = jnp.exp(2.0 * log_speed)
    factor = -stress / speed
    return [factor * t for t in tangent], 2.0 * log_speed


def first_kernel(
    velocity_ref, viscosity_ref, xa_ref, xb_ref, ya_ref, yb_ref, match_ref, dest_ref,
    base_ref, samples_ref, rank_ref, padded, split, picked,
):
    points = match_ref.shape[0] * match_ref.shape[1]
    cells = as_row(match_ref[...])
    samples = sample_at(velocity_ref, cells, split, picked)
    for c in range(3):
        samples_ref[c : c + 1, :] = samples[c]
    owners = as_row(dest_ref[...])
    devices = lax.axis_size("region") * lax.axis_size("blk")
    width = 128
    before = jnp.where(
        row_iota((width, width)) < lax.broadcasted_iota(jnp.int32, (width, width), 1), 1.0, 0.0
    )
    table = jnp.concatenate([before, jnp.ones((width, width), F32)], axis=0).astype(BF16)
    earlier = jnp.zeros((devices, width), F32)
    for start in range(0, points, width):
        hot = jnp.where(row_iota((devices, width)) == owners[:, start : start + width], 1.0, 0.0)
        both = jnp.concatenate([hot, earlier], axis=1).astype(BF16)
        running = jnp.dot(both, table, preferred_element_type=F32)
        rank_ref[0:1, start : start + width] = jnp.sum(hot * running, axis=0, keepdims=True)
        earlier = earlier + hot
    fill_padded(padded, velocity_ref, xa_ref, xb_ref, ya_ref, yb_ref)

    def emit(spot, here, change):
        base_ref[spot] = here + change

    stencil(padded, viscosity_ref, TIME_STEP, emit)


def faces_of(field_ref, xa_ref, xb_ref, ya_ref, yb_ref):
    comps, nx, ny, _ = field_ref.shape
    spot = jnp.where(even_side("region"), nx - 2, 0)
    even_y = even_side("blk")
    for c in range(comps):
        xa_ref[c] = field_ref[c, pl.ds(spot, 2)]
        xb_ref[c] = field_ref[c, pl.ds(nx - 2 - spot, 2)]
        low, high = field_ref[c, :, 0:2, :], field_ref[c, :, ny - 2 : ny, :]
        ya_ref[c] = jnp.where(even_y, high, low)
        yb_ref[c] = jnp.where(even_y, low, high)


def live_row(count_ref, points):
    return lax.broadcasted_iota(jnp.int32, (1, points), 1) < count_ref[0]


def stress_kernel(
    count_ref, arrived_ref, dest_ref, wall_ref, rank_ref, samples_ref, base_ref,
    first_ref, xa_ref, xb_ref, ya_ref, yb_ref, geometry_ref,
):
    comps, nx, ny, nz = base_ref.shape
    devices, fields = arrived_ref.shape
    capacity = fields // 4
    points = wall_ref.shape[0] * wall_ref.shape[1]
    owners = as_row(dest_ref[...])
    hot = jnp.where(row_iota((devices, points)) == owners, 1.0, 0.0).astype(BF16)
    table = None
    for part in pieces_of(arrived_ref[...], 3):
        term = lax.dot_general(
            part, hot, (((0,), (0,)), ((), ())), preferred_element_type=F32
        )
        table = term if table is None else table + term
    rank = rank_ref[0:1, :].astype(jnp.int32)
    mask = row_iota((capacity, points)) == rank
    rows = [
        jnp.sum(
            jnp.where(mask, table[k * capacity : (k + 1) * capacity, :], 0.0),
            axis=0, keepdims=True,
        )
        for k in range(4)
    ]
    distance = rows[0]
    length = jnp.sqrt(rows[1] * rows[1] + rows[2] * rows[2] + rows[3] * rows[3])
    normals = [row / length for row in rows[1:]]
    geometry_ref[0:1, :] = distance
    for k in range(3):
        geometry_ref[k + 1 : k + 2, :] = normals[k]
    samples = [samples_ref[c : c + 1, :] for c in range(3)]
    stress, _ = wall_solve(samples, distance, normals)
    live = live_row(count_ref, points)
    stress = [jnp.where(live, value, 0.0) for value in stress]
    force = scatter_sum(stress, as_row(wall_ref[...]), live, base_ref.shape)
    for c in range(comps):
        block = force[:, c * nz : (c + 1) * nz] * (TIME_STEP / WALL_DY)
        first_ref[c] = base_ref[c] + block.reshape(nx, ny, nz)
    faces_of(first_ref, xa_ref, xb_ref, ya_ref, yb_ref)


def second_kernel(
    count_ref, first_ref, match_ref, wall_ref, geometry_ref, force_ref, log_ref, split, picked,
):
    comps, nx, ny, nz = first_ref.shape
    points = wall_ref.shape[0] * wall_ref.shape[1]
    samples = sample_at(first_ref, as_row(match_ref[...]), split, picked)
    distance = geometry_ref[0:1, :]
    normals = [geometry_ref[k : k + 1, :] for k in range(1, 4)]
    stress, log_stress = wall_solve(samples, distance, normals)
    live = live_row(count_ref, points)
    log_stress = jnp.where(live, log_stress, 0.0)
    for i in range(log_ref.shape[0]):
        log_ref[i : i + 1, :] = log_stress[:, i * 128 : (i + 1) * 128]
    stress = [jnp.where(live, value, 0.0) for value in stress]
    force = scatter_sum(stress, as_row(wall_ref[...]), live, first_ref.shape)
    for c in range(comps):
        block = force[:, c * nz : (c + 1) * nz] * (0.5 * TIME_STEP / WALL_DY)
        force_ref[c] = block.reshape(nx, ny, nz)


def last_kernel(
    velocity_ref, viscosity_ref, first_ref, force_ref, xa_ref, xb_ref, ya_ref, yb_ref,
    advanced_ref, padded,
):
    fill_padded(padded, first_ref, xa_ref, xb_ref, ya_ref, yb_ref)

    def emit(spot, here, change):
        advanced_ref[spot] = 0.5 * (velocity_ref[spot] + here) + (change + force_ref[spot])

    stencil(padded, viscosity_ref, 0.5 * TIME_STEP, emit)


def exchange(faces):
    regions, blocks = lax.axis_size("region"), lax.axis_size("blk")

    def swap(block, partner):
        pairs = []
        for r in range(regions):
            for b in range(blocks):
                to_r, to_b = partner(r, b)
                pairs.append((r * blocks + b, to_r * blocks + to_b))
        return lax.ppermute(block, ("region", "blk"), pairs)

    def x_far(r, b):
        return (r, b ^ 1) if r in (0, regions - 1) else (((r - 1) ^ 1) + 1, b)

    def y_far(r, b):
        return (r ^ 1, b) if b in (0, blocks - 1) else (r, ((b - 1) ^ 1) + 1)

    xa, xb, ya, yb = faces
    return (
        swap(xa, lambda r, b: (r ^ 1, b)),
        swap(xb, x_far),
        swap(ya, lambda r, b: (r, b ^ 1)),
        swap(yb, y_far),
    )


def local(velocity, viscosity, match_cell, wall_cell, match_dest, match_count, wall_geom):
    devices = lax.axis_size("region") * lax.axis_size("blk")
    capacity = wall_geom.shape[1] // devices
    points = match_cell.shape[0]
    comps, nx, ny, nz = velocity.shape
    field = jax.ShapeDtypeStruct(velocity.shape, F32)
    xface = jax.ShapeDtypeStruct((comps, 2, ny, nz), F32)
    yface = jax.ShapeDtypeStruct((comps, nx, 2, nz), F32)
    rowed = jax.ShapeDtypeStruct((4, points), F32)
    square = (points // 128, 128)
    match = match_cell.reshape(square)
    wall = wall_cell.reshape(square)
    dest = match_dest.reshape(square)
    vmem = pl.BlockSpec(memory_space=pltpu.VMEM)
    limit = pltpu.CompilerParams(vmem_limit_bytes=24 * 1024 * 1024)
    smem = pl.BlockSpec(memory_space=pltpu.SMEM)
    padded = pltpu.VMEM((comps, nz // 128, nx + 4, ny + 16, 128), F32)
    split = pltpu.VMEM((comps * nx * ny, PIECES * nz), BF16)
    picked = pltpu.VMEM((comps * nx * ny, 256), F32)

    outgoing = wall_geom.reshape(4, devices, capacity).transpose(1, 0, 2).reshape(devices, -1)
    arrived = lax.all_to_all(outgoing, ("region", "blk"), split_axis=0, concat_axis=0, tiled=True)
    faces = pl.pallas_call(
        faces_of,
        out_shape=(xface, xface, yface, yface),
        in_specs=[vmem],
        out_specs=(vmem,) * 4,
        compiler_params=limit,
        name="faces",
    )(velocity)
    halos = exchange(faces)
    base, samples, rank = pl.pallas_call(
        first_kernel,
        out_shape=(field, rowed, jax.ShapeDtypeStruct((1, points), F32)),
        in_specs=[vmem] * 8,
        out_specs=(vmem,) * 3,
        scratch_shapes=[padded, split, picked],
        compiler_params=limit,
        name="first",
    )(velocity, viscosity, *halos, match, dest)
    first, *faces, geometry = pl.pallas_call(
        stress_kernel,
        out_shape=(field, xface, xface, yface, yface, rowed),
        in_specs=[smem] + [vmem] * 6,
        out_specs=(vmem,) * 6,
        compiler_params=limit,
        name="stress",
    )(match_count, arrived, dest, wall, rank, samples, base)
    halos = exchange(faces)
    force, log_stress = pl.pallas_call(
        second_kernel,
        out_shape=(field, jax.ShapeDtypeStruct(square, F32)),
        in_specs=[smem] + [vmem] * 4,
        out_specs=(vmem,) * 2,
        scratch_shapes=[split, picked],
        compiler_params=limit,
        name="second",
    )(match_count, first, match, wall, geometry)
    advanced = pl.pallas_call(
        last_kernel,
        out_shape=field,
        in_specs=[vmem] * 8,
        out_specs=vmem,
        scratch_shapes=[padded],
        compiler_params=limit,
        name="last",
    )(velocity, viscosity, first, force, *halos)
    return (advanced, log_stress.reshape(points))


def solution(mesh):
    placed = (
        P(None, "region", "blk", None),
        P("region", "blk", None),
        P(("region", "blk")),
        P(("region", "blk")),
        P(("region", "blk"), None),
        P(("region", "blk")),
        P(None, ("region", "blk")),
    )
    return jax.shard_map(
        local,
        mesh=mesh,
        in_specs=placed,
        out_specs=(P(None, "region", "blk", None), P(("region", "blk"))),
        check_vma=False,
    )
```

```python
import jax
import jax.numpy as jnp
from jax import lax
from jax.experimental import pallas as pl
from jax.experimental.pallas import tpu as pltpu
from jax.sharding import PartitionSpec as P

NEWTON = 2

KAPPA = 0.41
DAMPING = 26.0
NU_WALL = 0.0002
WALL_DY = 0.0005
TIME_STEP = 0.1
SPEED_FLOOR = 0.5
GUESS_RATIO = 14.0
ETAS = 32
PIECES = 2
UNROLL = 2
FIELD_LANES = 64
F32 = jnp.float32
BF16 = jnp.bfloat16


def pieces_of(values, count):
    parts = []
    rest = values
    for index in range(count):
        part = rest.astype(BF16)
        parts.append(part)
        if index + 1 < count:
            rest = rest - part.astype(F32)
    return parts


def as_row(block):
    rows = block.shape[0]
    return jnp.concatenate([block[i : i + 1, :] for i in range(rows)], axis=1)


def row_iota(shape):
    return lax.broadcasted_iota(jnp.int32, shape, 0)


def even_side(axis):
    return lax.axis_index(axis) % 2 == 0


def at_end(axis):
    place = lax.axis_index(axis)
    return (place == 0) | (place == lax.axis_size(axis) - 1)


def fill_padded(padded, field_ref, xa_ref, xb_ref, ya_ref, yb_ref):
    comps, nx, ny, nz = field_ref.shape
    even_x, even_y = even_side("region"), even_side("blk")
    end_x, end_y = at_end("region"), at_end("blk")
    spot_a = jnp.where(even_x, nx + 2, 0)
    spot_b = nx + 2 - spot_a
    for c in range(comps):
        near_x = xa_ref[c]
        far_x = jnp.where(end_x, 0.0, xb_ref[c])
        near_y = ya_ref[c]
        far_y = jnp.where(end_y, 0.0, yb_ref[c])
        low_y = jnp.where(even_y, far_y, near_y)
        high_y = jnp.where(even_y, near_y, far_y)
        for h in range(nz // 128):
            lanes = slice(128 * h, 128 * h + 128)
            padded[c, h, 2 : 2 + nx, 8 : 8 + ny, :] = field_ref[c, :, :, lanes]
            padded[c, h, pl.ds(spot_a, 2), 8 : 8 + ny, :] = near_x[:, :, lanes]
            padded[c, h, pl.ds(spot_b, 2), 8 : 8 + ny, :] = far_x[:, :, lanes]
            padded[c, h, 2 : 2 + nx, 6:8, :] = low_y[:, :, lanes]
            padded[c, h, 2 : 2 + nx, 8 + ny : 10 + ny, :] = high_y[:, :, lanes]


def stencil(padded, viscosity_ref, step, keep, emit, finish=None):
    comps, halves = padded.shape[:2]
    nx, ny, _ = viscosity_ref.shape
    lane = lax.broadcasted_iota(jnp.int32, (8, 128), 1)
    top = [lane < 127, lane < 126]
    bottom = [lane >= 1, lane >= 2]
    scale = step / 12.0

    def plane(x, carry):
        for tile in range(ny // 8):
            y = 8 + 8 * tile
            here = [
                [padded[c, h, x + 2, y : y + 8, :] for h in range(halves)] for c in range(comps)
            ]
            for h in range(halves):
                lanes = slice(128 * h, 128 * h + 128)
                visc = viscosity_ref[x, 8 * tile : 8 * tile + 8, lanes] * scale
                visc_near = 16.0 * visc
                center = keep - 90.0 * visc
                speed = [here[c][h] * scale for c in range(comps)]
                for c in range(comps):

                    def along_z(shift):
                        count = abs(shift)
                        rolled = pltpu.roll(here[c][h], (-shift) % 128, 1)
                        other = h + (1 if shift > 0 else -1)
                        if 0 <= other < halves:
                            rest = pltpu.roll(here[c][other], (-shift) % 128, 1)
                        else:
                            rest = 0.0
                        inside = top[count - 1] if shift > 0 else bottom[count - 1]
                        return jnp.where(inside, rolled, rest)

                    def at(axis, shift):
                        if axis == 0:
                            return padded[c, h, x + 2 + shift, y : y + 8, :]
                        if axis == 1:
                            return padded[c, h, x + 2, y + shift : y + shift + 8, :]
                        return along_z(shift)

                    for axis in range(3):
                        a1, b1, a2, b2 = (at(axis, shift) for shift in (1, -1, 2, -2))
                        slope = 8.0 * (a1 - b1) - (a2 - b2)
                        if axis == 0:
                            near, far = a1 + b1, a2 + b2
                            advect = speed[axis] * slope
                        else:
                            near, far = near + (a1 + b1), far + (a2 + b2)
                            advect = advect + speed[axis] * slope
                    rows = slice(8 * tile, 8 * tile + 8)
                    value = center * here[c][h] + visc_near * near - visc * far - advect
                    emit((c, x, rows, lanes), value)
        if finish is not None:
            finish(x)
        return carry

    lax.fori_loop(0, nx, plane, 0, unroll=UNROLL)


def sample_at(field_ref, cells, split, picked):
    comps, nx, ny, nz = field_ref.shape
    points = cells.shape[1]
    rows = nx * ny
    for c in range(comps):
        values = field_ref[c].reshape(rows, nz)
        for index, part in enumerate(pieces_of(values, PIECES)):
            split[c * rows : (c + 1) * rows, index * nz : (index + 1) * nz] = part
    lane_cell = cells & (nz - 1)
    row_cell = cells // nz
    width = 256
    sums = [[] for _ in range(comps)]
    for start in range(0, points, width):
        lanes = slice(start, start + width)
        hot = jnp.where(row_iota((nz, width)) == lane_cell[:, lanes], 1.0, 0.0).astype(BF16)
        hots = jnp.concatenate([hot] * PIECES, axis=0)
        picked[...] = jnp.dot(split[...], hots, preferred_element_type=F32)
        mask = row_iota((rows, width)) == row_cell[:, lanes]
        for c in range(comps):
            block = picked[c * rows : (c + 1) * rows, :]
            sums[c].append(jnp.sum(jnp.where(mask, block, 0.0), axis=0, keepdims=True))
    return [jnp.concatenate(parts, axis=1) for parts in sums]


def scatter_sum(stresses, cells, live, shape):
    comps, nx, ny, nz = shape
    points = cells.shape[1]
    rows = nx * ny
    lane_cell = cells & (nz - 1)
    row_cell = cells // nz
    hot = jnp.where(row_iota((rows, points)) == row_cell, 1.0, 0.0).astype(BF16)
    match = (row_iota((nz, points)) == lane_cell) & live
    total = None
    split = [pieces_of(value, PIECES) for value in stresses]
    for index in range(PIECES):
        spread = jnp.concatenate(
            [
                jnp.where(match, split[c][index].astype(F32), 0.0).astype(BF16)
                for c in range(comps)
            ],
            axis=0,
        )
        part = lax.dot_general(
            hot, spread, (((1,), (1,)), ((), ())), preferred_element_type=F32
        )
        total = part if total is None else total + part
    return total


def wall_solve(samples, distance, normals):
    points = distance.shape[1]
    normal_part = sum(s * n for s, n in zip(samples, normals))
    tangent = [s - normal_part * n for s, n in zip(samples, normals)]
    speed = jnp.maximum(jnp.sqrt(sum(t * t for t in tangent)), SPEED_FLOOR)
    target = jnp.log(speed)
    log_speed = target - jnp.log(jnp.full_like(target, GUESS_RATIO))
    index = row_iota((ETAS, points)).astype(F32)
    top = ETAS - 1.0
    eta = (index / top) * (index / top)
    upper = jnp.minimum(index + 1.0, top) / top
    lower = jnp.maximum(index - 1.0, 0.0) / top
    weight = 0.5 * (upper * upper - lower * lower)
    for _ in range(NEWTON):
        pace = jnp.exp(log_speed)
        height = eta * (distance * pace)
        decay = height * (1.0 / (NU_WALL * DAMPING))
        fade = jnp.exp(-decay)
        damp = 1.0 - fade
        mixing = KAPPA * height * damp
        share = weight / (NU_WALL + mixing * damp)
        growth = mixing * (damp + 2.0 * decay * fade)
        total = jnp.sum(share, axis=0, keepdims=True)
        change = jnp.sum(share * growth / (NU_WALL + mixing * damp), axis=0, keepdims=True)
        value = jnp.log(distance * pace * pace * total) - target
        log_speed = log_speed - value / (2.0 - change / total)
    stress = jnp.exp(2.0 * log_speed)
    factor = -stress / speed
    return [factor * t for t in tangent], 2.0 * log_speed


def sample_kernel(velocity_ref, match_ref, dest_ref, samples_ref, rank_ref, split, picked):
    points = match_ref.shape[0] * match_ref.shape[1]
    cells = as_row(match_ref[...])
    samples = sample_at(velocity_ref, cells, split, picked)
    for c in range(3):
        samples_ref[c : c + 1, :] = samples[c]
    owners = as_row(dest_ref[...])
    devices = lax.axis_size("region") * lax.axis_size("blk")
    width = 128
    before = jnp.where(
        row_iota((width, width)) < lax.broadcasted_iota(jnp.int32, (width, width), 1), 1.0, 0.0
    )
    table = jnp.concatenate([before, jnp.ones((width, width), F32)], axis=0).astype(BF16)
    earlier = jnp.zeros((devices, width), F32)
    for start in range(0, points, width):
        hot = jnp.where(row_iota((devices, width)) == owners[:, start : start + width], 1.0, 0.0)
        both = jnp.concatenate([hot, earlier], axis=1).astype(BF16)
        running = jnp.dot(both, table, preferred_element_type=F32)
        rank_ref[0:1, start : start + width] = jnp.sum(hot * running, axis=0, keepdims=True)
        earlier = earlier + hot


def rate_kernel(
    velocity_ref, viscosity_ref, xa_ref, xb_ref, ya_ref, yb_ref, base_ref, padded
):
    fill_padded(padded, velocity_ref, xa_ref, xb_ref, ya_ref, yb_ref)

    def emit(spot, value):
        base_ref[spot] = value

    stencil(padded, viscosity_ref, TIME_STEP, 1.0, emit)


def pair_spot(nx):
    return jnp.where(even_side("region"), nx - 2, 0)


def faces_kernel(velocity_ref, xa_ref, xb_ref, ya_ref, yb_ref, low, high, sems):
    comps, nx, ny, _ = velocity_ref.shape
    spot = pair_spot(nx)
    copies = [
        pltpu.make_async_copy(source, target, sems.at[index])
        for index, (source, target) in enumerate(
            (
                (velocity_ref.at[:, pl.ds(spot, 2)], xa_ref),
                (velocity_ref.at[:, pl.ds(nx - 2 - spot, 2)], xb_ref),
                (velocity_ref.at[:, :, 0:8, :], low),
                (velocity_ref.at[:, :, ny - 8 : ny, :], high),
            )
        )
    ]
    for copy in copies:
        copy.start()
    for copy in copies:
        copy.wait()
    even_y = even_side("blk")
    for c in range(comps):
        near, far = high[c, :, 6:8, :], low[c, :, 0:2, :]
        ya_ref[c] = jnp.where(even_y, near, far)
        yb_ref[c] = jnp.where(even_y, far, near)


def faces_of(field_ref, xa_ref, xb_ref, ya_ref, yb_ref):
    comps, nx, ny, _ = field_ref.shape
    spot = pair_spot(nx)
    even_y = even_side("blk")
    for c in range(comps):
        xa_ref[c] = field_ref[c, pl.ds(spot, 2)]
        xb_ref[c] = field_ref[c, pl.ds(nx - 2 - spot, 2)]
        low, high = field_ref[c, :, 0:2, :], field_ref[c, :, ny - 2 : ny, :]
        ya_ref[c] = jnp.where(even_y, high, low)
        yb_ref[c] = jnp.where(even_y, low, high)


def pack_kernel(geometry_ref, out_ref):
    fields, faces = geometry_ref.shape
    devices = out_ref.shape[0]
    capacity = faces // devices
    lane = lax.broadcasted_iota(jnp.int32, (8, 128), 1)
    for tile in range(devices // 8):
        rows = None
        for k in range(fields):
            line = geometry_ref[k : k + 1, 128 * tile : 128 * tile + 128]
            wide = jnp.broadcast_to(line, (8, 128))
            moved = pltpu.roll(wide, capacity, 1, stride=capacity, stride_axis=0)
            if k > 0:
                moved = pltpu.roll(moved, k * capacity, 1)
            rows = moved if rows is None else jnp.where(lane >= k * capacity, moved, rows)
        for i in range(8):
            out_ref[8 * tile + 7 - i : 8 * tile + 8 - i, :] = rows[i : i + 1, :]


def live_row(count_ref, points):
    return lax.broadcasted_iota(jnp.int32, (1, points), 1) < count_ref[0]


def stress_kernel(
    count_ref, arrived_ref, dest_ref, wall_ref, rank_ref, samples_ref, base_ref,
    first_ref, xa_ref, xb_ref, ya_ref, yb_ref, geometry_ref,
):
    comps, nx, ny, nz = base_ref.shape
    devices = arrived_ref.shape[0]
    capacity = FIELD_LANES // 4
    points = wall_ref.shape[0] * wall_ref.shape[1]
    owners = as_row(dest_ref[...])
    hot = jnp.where(row_iota((devices, points)) == owners, 1.0, 0.0).astype(BF16)
    table = None
    for part in pieces_of(arrived_ref[:, :FIELD_LANES], 3):
        term = lax.dot_general(
            part, hot, (((0,), (0,)), ((), ())), preferred_element_type=F32
        )
        table = term if table is None else table + term
    rank = rank_ref[0:1, :].astype(jnp.int32)
    mask = row_iota((capacity, points)) == rank
    rows = [
        jnp.sum(
            jnp.where(mask, table[k * capacity : (k + 1) * capacity, :], 0.0),
            axis=0, keepdims=True,
        )
        for k in range(4)
    ]
    distance = rows[0]
    length = jnp.sqrt(rows[1] * rows[1] + rows[2] * rows[2] + rows[3] * rows[3])
    normals = [row / length for row in rows[1:]]
    geometry_ref[0:1, :] = distance
    for k in range(3):
        geometry_ref[k + 1 : k + 2, :] = normals[k]
    samples = [samples_ref[c : c + 1, :] for c in range(3)]
    stress, _ = wall_solve(samples, distance, normals)
    live = live_row(count_ref, points)
    stress = [jnp.where(live, value, 0.0) for value in stress]
    force = scatter_sum(stress, as_row(wall_ref[...]), live, base_ref.shape)
    for c in range(comps):
        block = force[:, c * nz : (c + 1) * nz] * (TIME_STEP / WALL_DY)
        first_ref[c] = base_ref[c] + block.reshape(nx, ny, nz)
    faces_of(first_ref, xa_ref, xb_ref, ya_ref, yb_ref)


def second_kernel(
    count_ref, first_ref, match_ref, wall_ref, geometry_ref, force_ref, log_ref, split, picked,
):
    comps, nx, ny, nz = first_ref.shape
    points = wall_ref.shape[0] * wall_ref.shape[1]
    samples = sample_at(first_ref, as_row(match_ref[...]), split, picked)
    distance = geometry_ref[0:1, :]
    normals = [geometry_ref[k : k + 1, :] for k in range(1, 4)]
    stress, log_stress = wall_solve(samples, distance, normals)
    live = live_row(count_ref, points)
    log_stress = jnp.where(live, log_stress, 0.0)
    for i in range(log_ref.shape[0]):
        log_ref[i : i + 1, :] = log_stress[:, i * 128 : (i + 1) * 128]
    stress = [jnp.where(live, value, 0.0) for value in stress]
    force = scatter_sum(stress, as_row(wall_ref[...]), live, first_ref.shape)
    for c in range(comps):
        block = force[:, c * nz : (c + 1) * nz] * (0.5 * TIME_STEP / WALL_DY)
        force_ref[c] = block.reshape(nx, ny, nz)


def last_kernel(
    velocity_ref, viscosity_ref, first_ref, force_ref, xa_ref, xb_ref, ya_ref, yb_ref,
    advanced_ref, padded, result, sems,
):
    fill_padded(padded, first_ref, xa_ref, xb_ref, ya_ref, yb_ref)

    def emit(spot, value):
        result[spot] = value + (0.5 * velocity_ref[spot] + force_ref[spot])

    def copy_of(x):
        return pltpu.make_async_copy(
            result.at[:, pl.ds(x, 1)], advanced_ref.at[:, pl.ds(x, 1)], sems.at[x]
        )

    def finish(x):
        copy_of(x).start()

    stencil(padded, viscosity_ref, 0.5 * TIME_STEP, 0.5, emit, finish)

    def settle(x, carry):
        copy_of(x).wait()
        return carry

    lax.fori_loop(0, result.shape[1], settle, 0)


def exchange(faces):
    regions, blocks = lax.axis_size("region"), lax.axis_size("blk")

    def swap(block, partner):
        pairs = []
        for r in range(regions):
            for b in range(blocks):
                to_r, to_b = partner(r, b)
                pairs.append((r * blocks + b, to_r * blocks + to_b))
        return lax.ppermute(block, ("region", "blk"), pairs)

    def x_far(r, b):
        return (r, b ^ 1) if r in (0, regions - 1) else (((r - 1) ^ 1) + 1, b)

    def y_far(r, b):
        return (r ^ 1, b) if b in (0, blocks - 1) else (r, ((b - 1) ^ 1) + 1)

    xa, xb, ya, yb = faces
    return (
        swap(xa, lambda r, b: (r ^ 1, b)),
        swap(xb, x_far),
        swap(ya, lambda r, b: (r, b ^ 1)),
        swap(yb, y_far),
    )


def local(velocity, viscosity, match_cell, wall_cell, match_dest, match_count, wall_geom):
    devices = lax.axis_size("region") * lax.axis_size("blk")
    assert 4 * (wall_geom.shape[1] // devices) == FIELD_LANES
    points = match_cell.shape[0]
    comps, nx, ny, nz = velocity.shape
    field = jax.ShapeDtypeStruct(velocity.shape, F32)
    xface = jax.ShapeDtypeStruct((comps, 2, ny, nz), F32)
    yface = jax.ShapeDtypeStruct((comps, nx, 2, nz), F32)
    rowed = jax.ShapeDtypeStruct((4, points), F32)
    square = (points // 128, 128)
    match = match_cell.reshape(square)
    wall = wall_cell.reshape(square)
    dest = match_dest.reshape(square)
    vmem = pl.BlockSpec(memory_space=pltpu.VMEM)
    limit = pltpu.CompilerParams(vmem_limit_bytes=24 * 1024 * 1024)
    smem = pl.BlockSpec(memory_space=pltpu.SMEM)
    padded = pltpu.VMEM((comps, nz // 128, nx + 4, ny + 16, 128), F32)
    split = pltpu.VMEM((comps * nx * ny, PIECES * nz), BF16)
    picked = pltpu.VMEM((comps * nx * ny, 256), F32)

    outgoing = pl.pallas_call(
        pack_kernel,
        out_shape=jax.ShapeDtypeStruct((devices, 128), F32),
        in_specs=[vmem],
        out_specs=vmem,
        compiler_params=limit,
        name="pack",
    )(wall_geom)
    arrived = lax.all_to_all(
        outgoing.reshape(devices, 1, 128),
        ("region", "blk"), split_axis=0, concat_axis=0, tiled=True,
    ).reshape(devices, 128)
    edge = pltpu.VMEM((comps, nx, 8, nz), F32)
    faces = pl.pallas_call(
        faces_kernel,
        out_shape=(xface, xface, yface, yface),
        in_specs=[pl.BlockSpec(memory_space=pltpu.HBM)],
        out_specs=(vmem,) * 4,
        scratch_shapes=[edge, edge, pltpu.SemaphoreType.DMA((4,))],
        compiler_params=limit,
        name="faces",
    )(velocity)
    halos = exchange(faces)
    samples, rank = pl.pallas_call(
        sample_kernel,
        out_shape=(rowed, jax.ShapeDtypeStruct((1, points), F32)),
        in_specs=[vmem] * 3,
        out_specs=(vmem,) * 2,
        scratch_shapes=[split, picked],
        compiler_params=limit,
        name="sample",
    )(velocity, match, dest)
    base = pl.pallas_call(
        rate_kernel,
        out_shape=field,
        in_specs=[vmem] * 6,
        out_specs=vmem,
        scratch_shapes=[padded],
        compiler_params=limit,
        name="rate",
    )(velocity, viscosity, *halos)
    first, *faces, geometry = pl.pallas_call(
        stress_kernel,
        out_shape=(field, xface, xface, yface, yface, rowed),
        in_specs=[smem] + [vmem] * 6,
        out_specs=(vmem,) * 6,
        compiler_params=limit,
        name="stress",
    )(match_count, arrived, dest, wall, rank, samples, base)
    halos = exchange(faces)
    force, log_stress = pl.pallas_call(
        second_kernel,
        out_shape=(field, jax.ShapeDtypeStruct(square, F32)),
        in_specs=[smem] + [vmem] * 4,
        out_specs=(vmem,) * 2,
        scratch_shapes=[split, picked],
        compiler_params=limit,
        name="second",
    )(match_count, first, match, wall, geometry)
    advanced = pl.pallas_call(
        last_kernel,
        out_shape=field,
        in_specs=[vmem] * 8,
        out_specs=pl.BlockSpec(memory_space=pl.ANY),
        scratch_shapes=[
            padded, pltpu.VMEM(velocity.shape, F32), pltpu.SemaphoreType.DMA((nx,))
        ],
        compiler_params=limit,
        name="last",
    )(velocity, viscosity, first, force, *halos)
    return (advanced, log_stress.reshape(points))


def solution(mesh):
    placed = (
        P(None, "region", "blk", None),
        P("region", "blk", None),
        P(("region", "blk")),
        P(("region", "blk")),
        P(("region", "blk"), None),
        P(("region", "blk")),
        P(None, ("region", "blk")),
    )
    return jax.shard_map(
        local,
        mesh=mesh,
        in_specs=placed,
        out_specs=(P(None, "region", "blk", None), P(("region", "blk"))),
        check_vma=False,
    )
```

```python
import jax
import jax.numpy as jnp
from jax import lax
from jax.experimental import pallas as pl
from jax.experimental.pallas import tpu as pltpu
from jax.sharding import PartitionSpec as P

NEWTON = 2

KAPPA = 0.41
DAMPING = 26.0
NU_WALL = 0.0002
WALL_DY = 0.0005
TIME_STEP = 0.1
SPEED_FLOOR = 0.5
GUESS_RATIO = 14.0
ETAS = 32
PIECES = 2
UNROLL = 2
PACK_COST = 4_000_000_000
FIELD_LANES = 64
F32 = jnp.float32
BF16 = jnp.bfloat16


def pieces_of(values, count):
    parts = []
    rest = values
    for index in range(count):
        part = rest.astype(BF16)
        parts.append(part)
        if index + 1 < count:
            rest = rest - part.astype(F32)
    return parts


def as_row(block):
    rows = block.shape[0]
    return jnp.concatenate([block[i : i + 1, :] for i in range(rows)], axis=1)


def row_iota(shape):
    return lax.broadcasted_iota(jnp.int32, shape, 0)


def even_side(axis):
    return lax.axis_index(axis) % 2 == 0


def at_end(axis):
    place = lax.axis_index(axis)
    return (place == 0) | (place == lax.axis_size(axis) - 1)


def fill_padded(padded, field_ref, xa_ref, xb_ref, ya_ref, yb_ref):
    comps, nx, ny, nz = field_ref.shape
    even_x, even_y = even_side("region"), even_side("blk")
    end_x, end_y = at_end("region"), at_end("blk")
    spot_a = jnp.where(even_x, nx + 2, 0)
    spot_b = nx + 2 - spot_a
    for c in range(comps):
        near_x = xa_ref[c]
        far_x = jnp.where(end_x, 0.0, xb_ref[c])
        near_y = ya_ref[c]
        far_y = jnp.where(end_y, 0.0, yb_ref[c])
        low_y = jnp.where(even_y, far_y, near_y)
        high_y = jnp.where(even_y, near_y, far_y)
        for h in range(nz // 128):
            lanes = slice(128 * h, 128 * h + 128)
            padded[c, h, 2 : 2 + nx, 8 : 8 + ny, :] = field_ref[c, :, :, lanes]
            padded[c, h, pl.ds(spot_a, 2), 8 : 8 + ny, :] = near_x[:, :, lanes]
            padded[c, h, pl.ds(spot_b, 2), 8 : 8 + ny, :] = far_x[:, :, lanes]
            padded[c, h, 2 : 2 + nx, 6:8, :] = low_y[:, :, lanes]
            padded[c, h, 2 : 2 + nx, 8 + ny : 10 + ny, :] = high_y[:, :, lanes]


def stencil(padded, viscosity_ref, step, keep, emit, finish=None):
    comps, halves = padded.shape[:2]
    nx, ny, _ = viscosity_ref.shape
    lane = lax.broadcasted_iota(jnp.int32, (8, 128), 1)
    top = [lane < 127, lane < 126]
    bottom = [lane >= 1, lane >= 2]
    scale = step / 12.0

    def plane(x, carry):
        for tile in range(ny // 8):
            y = 8 + 8 * tile
            here = [
                [padded[c, h, x + 2, y : y + 8, :] for h in range(halves)] for c in range(comps)
            ]
            for h in range(halves):
                lanes = slice(128 * h, 128 * h + 128)
                visc = viscosity_ref[x, 8 * tile : 8 * tile + 8, lanes] * scale
                visc_near = 16.0 * visc
                center = keep - 90.0 * visc
                speed = [here[c][h] * scale for c in range(comps)]
                for c in range(comps):

                    def along_z(shift):
                        count = abs(shift)
                        rolled = pltpu.roll(here[c][h], (-shift) % 128, 1)
                        other = h + (1 if shift > 0 else -1)
                        if 0 <= other < halves:
                            rest = pltpu.roll(here[c][other], (-shift) % 128, 1)
                        else:
                            rest = 0.0
                        inside = top[count - 1] if shift > 0 else bottom[count - 1]
                        return jnp.where(inside, rolled, rest)

                    def at(axis, shift):
                        if axis == 0:
                            return padded[c, h, x + 2 + shift, y : y + 8, :]
                        if axis == 1:
                            return padded[c, h, x + 2, y + shift : y + shift + 8, :]
                        return along_z(shift)

                    for axis in range(3):
                        a1, b1, a2, b2 = (at(axis, shift) for shift in (1, -1, 2, -2))
                        slope = 8.0 * (a1 - b1) - (a2 - b2)
                        if axis == 0:
                            near, far = a1 + b1, a2 + b2
                            advect = speed[axis] * slope
                        else:
                            near, far = near + (a1 + b1), far + (a2 + b2)
                            advect = advect + speed[axis] * slope
                    rows = slice(8 * tile, 8 * tile + 8)
                    value = center * here[c][h] + visc_near * near - visc * far - advect
                    emit((c, x, rows, lanes), value)
        if finish is not None:
            finish(x)
        return carry

    lax.fori_loop(0, nx, plane, 0, unroll=UNROLL)


def sample_at(field_ref, rows_ref, turns_ref, tiles):
    comps, nx, ny, nz = field_ref.shape
    for c in range(comps):
        for x in range(nx):
            for y in range(0, ny, 8):
                for h in range(nz // 128):
                    start = ((h * nx + x) * ny + y) * 8 + c
                    tiles[pl.ds(start, 8, stride=8), :] = field_ref[
                        c, x, y : y + 8, 128 * h : 128 * h + 128
                    ]
    lane = lax.broadcasted_iota(jnp.int32, (8, 128), 1)
    blocks = []
    for start in range(0, rows_ref.shape[0], 128):
        parts = []
        for low in range(0, 128, 32):
            part = jnp.zeros((8, 128), F32)
            for spot in range(low, low + 32):
                row = pl.multiple_of(rows_ref[start + spot], 8)
                turned = pltpu.roll(tiles[pl.ds(row, 8), :], turns_ref[start + spot], 1)
                part = jnp.where(lane == spot, turned, part)
            parts.append(part)
        blocks.append((parts[0] + parts[1]) + (parts[2] + parts[3]))
    return [jnp.concatenate([block[c : c + 1] for block in blocks], axis=1) for c in range(comps)]


def scatter_sum(stresses, cells, live, shape):
    comps, nx, ny, nz = shape
    points = cells.shape[1]
    rows = nx * ny
    lane_cell = cells & (nz - 1)
    row_cell = cells // nz
    hot = jnp.where(row_iota((rows, points)) == row_cell, 1.0, 0.0).astype(BF16)
    match = (row_iota((nz, points)) == lane_cell) & live
    total = None
    split = [pieces_of(value, PIECES) for value in stresses]
    for index in range(PIECES):
        spread = jnp.concatenate(
            [
                jnp.where(match, split[c][index].astype(F32), 0.0).astype(BF16)
                for c in range(comps)
            ],
            axis=0,
        )
        part = lax.dot_general(
            hot, spread, (((1,), (1,)), ((), ())), preferred_element_type=F32
        )
        total = part if total is None else total + part
    return total


def wall_solve(samples, distance, normals):
    points = distance.shape[1]
    normal_part = sum(s * n for s, n in zip(samples, normals))
    tangent = [s - normal_part * n for s, n in zip(samples, normals)]
    speed = jnp.maximum(jnp.sqrt(sum(t * t for t in tangent)), SPEED_FLOOR)
    target = jnp.log(speed)
    log_speed = target - jnp.log(jnp.full_like(target, GUESS_RATIO))
    index = row_iota((ETAS, points)).astype(F32)
    top = ETAS - 1.0
    eta = (index / top) * (index / top)
    upper = jnp.minimum(index + 1.0, top) / top
    lower = jnp.maximum(index - 1.0, 0.0) / top
    weight = 0.5 * (upper * upper - lower * lower)
    for _ in range(NEWTON):
        pace = jnp.exp(log_speed)
        height = eta * (distance * pace)
        decay = height * (1.0 / (NU_WALL * DAMPING))
        fade = jnp.exp(-decay)
        damp = 1.0 - fade
        mixing = KAPPA * height * damp
        share = weight / (NU_WALL + mixing * damp)
        growth = mixing * (damp + 2.0 * decay * fade)
        total = jnp.sum(share, axis=0, keepdims=True)
        change = jnp.sum(share * growth / (NU_WALL + mixing * damp), axis=0, keepdims=True)
        value = jnp.log(distance * pace * pace * total) - target
        log_speed = log_speed - value / (2.0 - change / total)
    stress = jnp.exp(2.0 * log_speed)
    factor = -stress / speed
    return [factor * t for t in tangent], 2.0 * log_speed


def sample_kernel(rows_ref, turns_ref, velocity_ref, dest_ref, samples_ref, rank_ref, tiles):
    points = rows_ref.shape[0]
    samples = sample_at(velocity_ref, rows_ref, turns_ref, tiles)
    for c in range(3):
        samples_ref[c : c + 1, :] = samples[c]
    owners = as_row(dest_ref[...])
    devices = lax.axis_size("region") * lax.axis_size("blk")
    width = 128
    before = jnp.where(
        row_iota((width, width)) < lax.broadcasted_iota(jnp.int32, (width, width), 1), 1.0, 0.0
    )
    table = jnp.concatenate([before, jnp.ones((width, width), F32)], axis=0).astype(BF16)
    earlier = jnp.zeros((devices, width), F32)
    for start in range(0, points, width):
        hot = jnp.where(row_iota((devices, width)) == owners[:, start : start + width], 1.0, 0.0)
        both = jnp.concatenate([hot, earlier], axis=1).astype(BF16)
        running = jnp.dot(both, table, preferred_element_type=F32)
        rank_ref[0:1, start : start + width] = jnp.sum(hot * running, axis=0, keepdims=True)
        earlier = earlier + hot


def rate_kernel(
    velocity_ref, viscosity_ref, xa_ref, xb_ref, ya_ref, yb_ref, base_ref, padded
):
    fill_padded(padded, velocity_ref, xa_ref, xb_ref, ya_ref, yb_ref)

    def emit(spot, value):
        base_ref[spot] = value

    stencil(padded, viscosity_ref, TIME_STEP, 1.0, emit)


def pair_spot(nx):
    return jnp.where(even_side("region"), nx - 2, 0)


def faces_kernel(
    velocity_ref, match_ref, xa_ref, xb_ref, ya_ref, yb_ref, rows_ref, turns_ref
):
    _, nx, ny, nz = velocity_ref.shape
    cells = match_ref[...]
    half, row = (cells // 128) % (nz // 128), cells // nz
    rows_ref[...] = (half * (nx * ny) + row) * 8
    turns_ref[...] = (lax.broadcasted_iota(jnp.int32, cells.shape, 1) - cells) & 127
    faces_of(velocity_ref, xa_ref, xb_ref, ya_ref, yb_ref)


def faces_of(field_ref, xa_ref, xb_ref, ya_ref, yb_ref):
    comps, nx, ny, _ = field_ref.shape
    spot = pair_spot(nx)
    even_y = even_side("blk")
    for c in range(comps):
        xa_ref[c] = field_ref[c, pl.ds(spot, 2)]
        xb_ref[c] = field_ref[c, pl.ds(nx - 2 - spot, 2)]
        low, high = field_ref[c, :, 0:2, :], field_ref[c, :, ny - 2 : ny, :]
        ya_ref[c] = jnp.where(even_y, high, low)
        yb_ref[c] = jnp.where(even_y, low, high)


def pack_kernel(geometry_ref, out_ref):
    fields, faces = geometry_ref.shape
    devices = out_ref.shape[0]
    capacity = faces // devices
    lane = lax.broadcasted_iota(jnp.int32, (8, 128), 1)
    for tile in range(devices // 8):
        rows = None
        for k in range(fields):
            line = geometry_ref[k : k + 1, 128 * tile : 128 * tile + 128]
            wide = jnp.broadcast_to(line, (8, 128))
            moved = pltpu.roll(wide, capacity, 1, stride=capacity, stride_axis=0)
            if k > 0:
                moved = pltpu.roll(moved, k * capacity, 1)
            rows = moved if rows is None else jnp.where(lane >= k * capacity, moved, rows)
        for i in range(8):
            out_ref[8 * tile + 7 - i : 8 * tile + 8 - i, :] = rows[i : i + 1, :]


def live_row(count_ref, points):
    return lax.broadcasted_iota(jnp.int32, (1, points), 1) < count_ref[0]


def stress_kernel(
    count_ref, arrived_ref, dest_ref, wall_ref, rank_ref, samples_ref, base_ref,
    first_ref, xa_ref, xb_ref, ya_ref, yb_ref, geometry_ref,
):
    comps, nx, ny, nz = base_ref.shape
    devices = arrived_ref.shape[0]
    capacity = FIELD_LANES // 4
    points = wall_ref.shape[0] * wall_ref.shape[1]
    owners = as_row(dest_ref[...])
    hot = jnp.where(row_iota((devices, points)) == owners, 1.0, 0.0).astype(BF16)
    table = None
    for part in pieces_of(arrived_ref[:, :FIELD_LANES], 3):
        term = lax.dot_general(
            part, hot, (((0,), (0,)), ((), ())), preferred_element_type=F32
        )
        table = term if table is None else table + term
    rank = rank_ref[0:1, :].astype(jnp.int32)
    mask = row_iota((capacity, points)) == rank
    rows = [
        jnp.sum(
            jnp.where(mask, table[k * capacity : (k + 1) * capacity, :], 0.0),
            axis=0, keepdims=True,
        )
        for k in range(4)
    ]
    distance = rows[0]
    length = jnp.sqrt(rows[1] * rows[1] + rows[2] * rows[2] + rows[3] * rows[3])
    normals = [row / length for row in rows[1:]]
    geometry_ref[0:1, :] = distance
    for k in range(3):
        geometry_ref[k + 1 : k + 2, :] = normals[k]
    samples = [samples_ref[c : c + 1, :] for c in range(3)]
    stress, _ = wall_solve(samples, distance, normals)
    live = live_row(count_ref, points)
    stress = [jnp.where(live, value, 0.0) for value in stress]
    force = scatter_sum(stress, as_row(wall_ref[...]), live, base_ref.shape)
    for c in range(comps):
        block = force[:, c * nz : (c + 1) * nz] * (TIME_STEP / WALL_DY)
        first_ref[c] = base_ref[c] + block.reshape(nx, ny, nz)
    faces_of(first_ref, xa_ref, xb_ref, ya_ref, yb_ref)


def second_kernel(
    count_ref, rows_ref, turns_ref, velocity_ref, first_ref, wall_ref, geometry_ref,
    part_ref, log_ref, tiles,
):
    comps, nx, ny, nz = first_ref.shape
    points = rows_ref.shape[0]
    samples = sample_at(first_ref, rows_ref, turns_ref, tiles)
    distance = geometry_ref[0:1, :]
    normals = [geometry_ref[k : k + 1, :] for k in range(1, 4)]
    stress, log_stress = wall_solve(samples, distance, normals)
    live = live_row(count_ref, points)
    log_stress = jnp.where(live, log_stress, 0.0)
    for i in range(log_ref.shape[0]):
        log_ref[i : i + 1, :] = log_stress[:, i * 128 : (i + 1) * 128]
    stress = [jnp.where(live, value, 0.0) for value in stress]
    force = scatter_sum(stress, as_row(wall_ref[...]), live, first_ref.shape)
    for c in range(comps):
        block = force[:, c * nz : (c + 1) * nz] * (0.5 * TIME_STEP / WALL_DY)
        part_ref[c] = 0.5 * velocity_ref[c] + block.reshape(nx, ny, nz)


def last_kernel(
    viscosity_ref, first_ref, part_ref, xa_ref, xb_ref, ya_ref, yb_ref,
    advanced_ref, padded, result, sems,
):
    fill_padded(padded, first_ref, xa_ref, xb_ref, ya_ref, yb_ref)

    def emit(spot, value):
        result[spot] = value + part_ref[spot]

    def copy_of(x):
        return pltpu.make_async_copy(
            result.at[:, pl.ds(x, 1)], advanced_ref.at[:, pl.ds(x, 1)], sems.at[x]
        )

    def finish(x):
        copy_of(x).start()

    stencil(padded, viscosity_ref, 0.5 * TIME_STEP, 0.5, emit, finish)

    def settle(x, carry):
        copy_of(x).wait()
        return carry

    lax.fori_loop(0, result.shape[1], settle, 0)


def exchange(faces):
    regions, blocks = lax.axis_size("region"), lax.axis_size("blk")

    def swap(block, partner):
        pairs = []
        for r in range(regions):
            for b in range(blocks):
                to_r, to_b = partner(r, b)
                pairs.append((r * blocks + b, to_r * blocks + to_b))
        return lax.ppermute(block, ("region", "blk"), pairs)

    def x_far(r, b):
        return (r, b ^ 1) if r in (0, regions - 1) else (((r - 1) ^ 1) + 1, b)

    def y_far(r, b):
        return (r ^ 1, b) if b in (0, blocks - 1) else (r, ((b - 1) ^ 1) + 1)

    xa, xb, ya, yb = faces
    return (
        swap(xa, lambda r, b: (r ^ 1, b)),
        swap(xb, x_far),
        swap(ya, lambda r, b: (r, b ^ 1)),
        swap(yb, y_far),
    )


def local(velocity, viscosity, match_cell, wall_cell, match_dest, match_count, wall_geom):
    devices = lax.axis_size("region") * lax.axis_size("blk")
    assert 4 * (wall_geom.shape[1] // devices) == FIELD_LANES
    points = match_cell.shape[0]
    comps, nx, ny, nz = velocity.shape
    field = jax.ShapeDtypeStruct(velocity.shape, F32)
    xface = jax.ShapeDtypeStruct((comps, 2, ny, nz), F32)
    yface = jax.ShapeDtypeStruct((comps, nx, 2, nz), F32)
    rowed = jax.ShapeDtypeStruct((4, points), F32)
    square = (points // 128, 128)
    match = match_cell.reshape(square)
    wall = wall_cell.reshape(square)
    dest = match_dest.reshape(square)
    vmem = pl.BlockSpec(memory_space=pltpu.VMEM)
    limit = pltpu.CompilerParams(vmem_limit_bytes=24 * 1024 * 1024)
    smem = pl.BlockSpec(memory_space=pltpu.SMEM)
    padded = pltpu.VMEM((comps, nz // 128, nx + 4, ny + 16, 128), F32)
    tiles = pltpu.VMEM((8 * nx * ny * (nz // 128), 128), F32)

    spots = jax.ShapeDtypeStruct(square, jnp.int32)
    outgoing = pl.pallas_call(
        pack_kernel,
        out_shape=jax.ShapeDtypeStruct((devices, 128), F32),
        in_specs=[vmem],
        out_specs=vmem,
        compiler_params=limit,
        cost_estimate=pl.CostEstimate(flops=PACK_COST, bytes_accessed=98304, transcendentals=0),
        name="pack",
    )(wall_geom)
    arrived = lax.all_to_all(
        outgoing.reshape(devices, 1, 128),
        ("region", "blk"), split_axis=0, concat_axis=0, tiled=True,
    ).reshape(devices, 128)
    *faces, rows, turns = pl.pallas_call(
        faces_kernel,
        out_shape=(xface, xface, yface, yface, spots, spots),
        in_specs=[vmem] * 2,
        out_specs=(vmem,) * 6,
        compiler_params=limit,
        name="faces",
    )(velocity, match)
    rows, turns = rows.reshape(points), turns.reshape(points)
    halos = exchange(faces)
    samples, rank = pl.pallas_call(
        sample_kernel,
        out_shape=(rowed, jax.ShapeDtypeStruct((1, points), F32)),
        in_specs=[smem] * 2 + [vmem] * 2,
        out_specs=(vmem,) * 2,
        scratch_shapes=[tiles],
        compiler_params=limit,
        name="sample",
    )(rows, turns, velocity, dest)
    base = pl.pallas_call(
        rate_kernel,
        out_shape=field,
        in_specs=[vmem] * 6,
        out_specs=vmem,
        scratch_shapes=[padded],
        compiler_params=limit,
        name="rate",
    )(velocity, viscosity, *halos)
    first, *faces, geometry = pl.pallas_call(
        stress_kernel,
        out_shape=(field, xface, xface, yface, yface, rowed),
        in_specs=[smem] + [vmem] * 6,
        out_specs=(vmem,) * 6,
        compiler_params=limit,
        name="stress",
    )(match_count, arrived, dest, wall, rank, samples, base)
    halos = exchange(faces)
    part, log_stress = pl.pallas_call(
        second_kernel,
        out_shape=(field, jax.ShapeDtypeStruct(square, F32)),
        in_specs=[smem] * 3 + [vmem] * 4,
        out_specs=(vmem,) * 2,
        scratch_shapes=[tiles],
        compiler_params=limit,
        name="second",
    )(match_count, rows, turns, velocity, first, wall, geometry)
    advanced = pl.pallas_call(
        last_kernel,
        out_shape=field,
        in_specs=[vmem] * 7,
        out_specs=pl.BlockSpec(memory_space=pl.ANY),
        scratch_shapes=[
            padded, pltpu.VMEM(velocity.shape, F32), pltpu.SemaphoreType.DMA((nx,))
        ],
        compiler_params=limit,
        name="last",
    )(viscosity, first, part, *halos)
    return (advanced, log_stress.reshape(points))


def solution(mesh):
    placed = (
        P(None, "region", "blk", None),
        P("region", "blk", None),
        P(("region", "blk")),
        P(("region", "blk")),
        P(("region", "blk"), None),
        P(("region", "blk")),
        P(None, ("region", "blk")),
    )
    return jax.shard_map(
        local,
        mesh=mesh,
        in_specs=placed,
        out_specs=(P(None, "region", "blk", None), P(("region", "blk"))),
        check_vma=False,
    )
```

```python
import math

import jax
import jax.numpy as jnp
from jax import lax
from jax.experimental import pallas as pl
from jax.experimental.pallas import tpu as pltpu
from jax.sharding import PartitionSpec as P

NEWTON = 2

KAPPA = 0.41
DAMPING = 26.0
NU_WALL = 0.0002
WALL_DY = 0.0005
TIME_STEP = 0.1
SPEED_FLOOR = 0.5
GUESS_RATIO = 14.0
ETAS = 32
PIECES = 2
UNROLL = 4
TILE_ROWS = 3
PACK_COST = 4_000_000_000
FIELD_LANES = 64
F32 = jnp.float32
BF16 = jnp.bfloat16


def pieces_of(values, count):
    parts = []
    rest = values
    for index in range(count):
        part = rest.astype(BF16)
        parts.append(part)
        if index + 1 < count:
            rest = rest - part.astype(F32)
    return parts


def as_row(block):
    rows = block.shape[0]
    return jnp.concatenate([block[i : i + 1, :] for i in range(rows)], axis=1)


def row_iota(shape):
    return lax.broadcasted_iota(jnp.int32, shape, 0)


def even_side(axis):
    return lax.axis_index(axis) % 2 == 0


def at_end(axis):
    place = lax.axis_index(axis)
    return (place == 0) | (place == lax.axis_size(axis) - 1)


def fill_padded(padded, field_ref, xa_ref, xb_ref, ya_ref, yb_ref):
    comps, nx, ny, nz = field_ref.shape
    even_x, even_y = even_side("region"), even_side("blk")
    end_x, end_y = at_end("region"), at_end("blk")
    spot_a = jnp.where(even_x, nx + 2, 0)
    spot_b = nx + 2 - spot_a
    for c in range(comps):
        near_x = xa_ref[c]
        far_x = jnp.where(end_x, 0.0, xb_ref[c])
        near_y = ya_ref[c]
        far_y = jnp.where(end_y, 0.0, yb_ref[c])
        low_y = jnp.where(even_y, far_y, near_y)
        high_y = jnp.where(even_y, near_y, far_y)
        for h in range(nz // 128):
            lanes = slice(128 * h, 128 * h + 128)
            padded[c, h, 2 : 2 + nx, 8 : 8 + ny, :] = field_ref[c, :, :, lanes]
            padded[c, h, pl.ds(spot_a, 2), 8 : 8 + ny, :] = near_x[:, :, lanes]
            padded[c, h, pl.ds(spot_b, 2), 8 : 8 + ny, :] = far_x[:, :, lanes]
            padded[c, h, 2 : 2 + nx, 6:8, :] = low_y[:, :, lanes]
            padded[c, h, 2 : 2 + nx, 8 + ny : 10 + ny, :] = high_y[:, :, lanes]


def stencil(padded, viscosity_ref, step, keep, emit, finish=None):
    comps, halves = padded.shape[:2]
    nx, ny, _ = viscosity_ref.shape
    lane = lax.broadcasted_iota(jnp.int32, (8, 128), 1)
    top = [lane < 127, lane < 126]
    bottom = [lane >= 1, lane >= 2]
    scale = step / 12.0

    def plane(x, carry):
        for tile in range(ny // 8):
            y = 8 + 8 * tile
            here = [
                [padded[c, h, x + 2, y : y + 8, :] for h in range(halves)] for c in range(comps)
            ]
            for h in range(halves):
                lanes = slice(128 * h, 128 * h + 128)
                visc = viscosity_ref[x, 8 * tile : 8 * tile + 8, lanes] * scale
                visc_near = 16.0 * visc
                center = keep - 90.0 * visc
                speed = [here[c][h] * scale for c in range(comps)]
                for c in range(comps):

                    def along_z(shift):
                        count = abs(shift)
                        rolled = pltpu.roll(here[c][h], (-shift) % 128, 1)
                        other = h + (1 if shift > 0 else -1)
                        if 0 <= other < halves:
                            rest = pltpu.roll(here[c][other], (-shift) % 128, 1)
                        else:
                            rest = 0.0
                        inside = top[count - 1] if shift > 0 else bottom[count - 1]
                        return jnp.where(inside, rolled, rest)

                    def at(axis, shift):
                        if axis == 0:
                            return padded[c, h, x + 2 + shift, y : y + 8, :]
                        if axis == 1:
                            return padded[c, h, x + 2, y + shift : y + shift + 8, :]
                        return along_z(shift)

                    for axis in range(3):
                        a1, b1, a2, b2 = (at(axis, shift) for shift in (1, -1, 2, -2))
                        slope = 8.0 * (a1 - b1) - (a2 - b2)
                        if axis == 0:
                            near, far = a1 + b1, a2 + b2
                            advect = speed[axis] * slope
                        else:
                            near, far = near + (a1 + b1), far + (a2 + b2)
                            advect = advect + speed[axis] * slope
                    rows = slice(8 * tile, 8 * tile + 8)
                    value = center * here[c][h] + visc_near * near - visc * far - advect
                    emit((c, x, rows, lanes), value)
        if finish is not None:
            finish(x)
        return carry

    lax.fori_loop(0, nx, plane, 0, unroll=UNROLL)


def sample_at(field_ref, rows_ref, turns_ref, tiles):
    comps, nx, ny, nz = field_ref.shape
    for c in range(comps):
        for x in range(nx):
            for y in range(0, ny, 8):
                for h in range(nz // 128):
                    start = ((h * nx + x) * ny + y) * TILE_ROWS + c
                    tiles[pl.ds(start, 8, stride=TILE_ROWS), :] = field_ref[
                        c, x, y : y + 8, 128 * h : 128 * h + 128
                    ]
    lane = lax.broadcasted_iota(jnp.int32, (8, 128), 1)
    blocks = []
    for start in range(0, rows_ref.shape[0], 128):
        parts = []
        for low in range(0, 128, 32):
            part = jnp.zeros((8, 128), F32)
            for spot in range(low, low + 32):
                row = rows_ref[start + spot]
                turned = pltpu.roll(tiles[pl.ds(row, 8), :], turns_ref[start + spot], 1)
                part = jnp.where(lane == spot, turned, part)
            parts.append(part)
        blocks.append((parts[0] + parts[1]) + (parts[2] + parts[3]))
    return [jnp.concatenate([block[c : c + 1] for block in blocks], axis=1) for c in range(comps)]


def scatter_sum(stresses, cells, live, shape):
    comps, nx, ny, nz = shape
    points = cells.shape[1]
    rows = nx * ny
    lane_cell = cells & (nz - 1)
    row_cell = cells // nz
    hot = jnp.where(row_iota((rows, points)) == row_cell, 1.0, 0.0).astype(BF16)
    match = (row_iota((nz, points)) == lane_cell) & live
    total = None
    split = [pieces_of(value, PIECES) for value in stresses]
    for index in range(PIECES):
        spread = jnp.concatenate(
            [
                jnp.where(match, split[c][index].astype(F32), 0.0).astype(BF16)
                for c in range(comps)
            ],
            axis=0,
        )
        part = lax.dot_general(
            hot, spread, (((1,), (1,)), ((), ())), preferred_element_type=F32
        )
        total = part if total is None else total + part
    return total


def wall_solve(samples, distance, normals):
    points = distance.shape[1]
    normal_part = sum(s * n for s, n in zip(samples, normals))
    tangent = [s - normal_part * n for s, n in zip(samples, normals)]
    speed = jnp.maximum(jnp.sqrt(sum(t * t for t in tangent)), SPEED_FLOOR)
    target = jnp.log(speed)
    log_speed = target - math.log(GUESS_RATIO)
    index = row_iota((ETAS, points)).astype(F32)
    top = ETAS - 1.0
    eta = (index / top) * (index / top)
    upper = jnp.minimum(index + 1.0, top) / top
    lower = jnp.maximum(index - 1.0, 0.0) / top
    weight = 0.5 * (upper * upper - lower * lower)
    for _ in range(NEWTON):
        pace = jnp.exp(log_speed)
        height = eta * (distance * pace)
        decay = height * (1.0 / (NU_WALL * DAMPING))
        fade = jnp.exp(-decay)
        damp = 1.0 - fade
        mixing = KAPPA * height * damp
        inverse = 1.0 / (NU_WALL + mixing * damp)
        growth = mixing * (damp + 2.0 * decay * fade)
        share = weight * inverse
        total = jnp.sum(share, axis=0, keepdims=True)
        change = jnp.sum(share * (growth * inverse), axis=0, keepdims=True)
        value = jnp.log(distance * pace * pace * total) - target
        log_speed = log_speed - value / (2.0 - change / total)
    stress = jnp.exp(2.0 * log_speed)
    factor = -stress / speed
    return [factor * t for t in tangent], 2.0 * log_speed


def sample_kernel(rows_ref, turns_ref, velocity_ref, dest_ref, samples_ref, rank_ref, tiles):
    points = rows_ref.shape[0]
    samples = sample_at(velocity_ref, rows_ref, turns_ref, tiles)
    for c in range(3):
        samples_ref[c : c + 1, :] = samples[c]
    owners = as_row(dest_ref[...])
    devices = lax.axis_size("region") * lax.axis_size("blk")
    width = 128
    before = jnp.where(
        row_iota((width, width)) < lax.broadcasted_iota(jnp.int32, (width, width), 1), 1.0, 0.0
    )
    table = jnp.concatenate([before, jnp.ones((width, width), F32)], axis=0).astype(BF16)
    earlier = jnp.zeros((devices, width), F32)
    for start in range(0, points, width):
        hot = jnp.where(row_iota((devices, width)) == owners[:, start : start + width], 1.0, 0.0)
        both = jnp.concatenate([hot, earlier], axis=1).astype(BF16)
        running = jnp.dot(both, table, preferred_element_type=F32)
        rank_ref[0:1, start : start + width] = jnp.sum(hot * running, axis=0, keepdims=True)
        earlier = earlier + hot


def rate_kernel(
    velocity_ref, viscosity_ref, xa_ref, xb_ref, ya_ref, yb_ref, base_ref, padded
):
    fill_padded(padded, velocity_ref, xa_ref, xb_ref, ya_ref, yb_ref)

    def emit(spot, value):
        base_ref[spot] = value

    stencil(padded, viscosity_ref, TIME_STEP, 1.0, emit)


def pair_spot(nx):
    return jnp.where(even_side("region"), nx - 2, 0)


def faces_kernel(
    velocity_ref, match_ref, xa_ref, xb_ref, ya_ref, yb_ref, rows_ref, turns_ref
):
    _, nx, ny, nz = velocity_ref.shape
    cells = match_ref[...]
    half, row = (cells // 128) % (nz // 128), cells // nz
    rows_ref[...] = (half * (nx * ny) + row) * TILE_ROWS
    turns_ref[...] = (lax.broadcasted_iota(jnp.int32, cells.shape, 1) - cells) & 127
    faces_of(velocity_ref, xa_ref, xb_ref, ya_ref, yb_ref)


def faces_of(field_ref, xa_ref, xb_ref, ya_ref, yb_ref):
    comps, nx, ny, _ = field_ref.shape
    spot = pair_spot(nx)
    even_y = even_side("blk")
    for c in range(comps):
        xa_ref[c] = field_ref[c, pl.ds(spot, 2)]
        xb_ref[c] = field_ref[c, pl.ds(nx - 2 - spot, 2)]
        low, high = field_ref[c, :, 0:2, :], field_ref[c, :, ny - 2 : ny, :]
        ya_ref[c] = jnp.where(even_y, high, low)
        yb_ref[c] = jnp.where(even_y, low, high)


def pack_kernel(geometry_ref, out_ref):
    fields, faces = geometry_ref.shape
    devices = out_ref.shape[0]
    capacity = faces // devices
    lane = lax.broadcasted_iota(jnp.int32, (8, 128), 1)
    for tile in range(devices // 8):
        rows = None
        for k in range(fields):
            line = geometry_ref[k : k + 1, 128 * tile : 128 * tile + 128]
            wide = jnp.broadcast_to(line, (8, 128))
            moved = pltpu.roll(wide, capacity, 1, stride=capacity, stride_axis=0)
            if k > 0:
                moved = pltpu.roll(moved, k * capacity, 1)
            rows = moved if rows is None else jnp.where(lane >= k * capacity, moved, rows)
        for i in range(8):
            out_ref[8 * tile + 7 - i : 8 * tile + 8 - i, :] = rows[i : i + 1, :]


def live_row(count_ref, points):
    return lax.broadcasted_iota(jnp.int32, (1, points), 1) < count_ref[0]


def stress_kernel(
    count_ref, arrived_ref, dest_ref, wall_ref, rank_ref, samples_ref, base_ref,
    first_ref, xa_ref, xb_ref, ya_ref, yb_ref, geometry_ref,
):
    comps, nx, ny, nz = base_ref.shape
    devices = arrived_ref.shape[0]
    capacity = FIELD_LANES // 4
    points = wall_ref.shape[0] * wall_ref.shape[1]
    owners = as_row(dest_ref[...])
    hot = jnp.where(row_iota((devices, points)) == owners, 1.0, 0.0).astype(BF16)
    table = None
    for part in pieces_of(arrived_ref[:, :FIELD_LANES], 3):
        term = lax.dot_general(
            part, hot, (((0,), (0,)), ((), ())), preferred_element_type=F32
        )
        table = term if table is None else table + term
    rank = rank_ref[0:1, :].astype(jnp.int32)
    mask = row_iota((capacity, points)) == rank
    rows = [
        jnp.sum(
            jnp.where(mask, table[k * capacity : (k + 1) * capacity, :], 0.0),
            axis=0, keepdims=True,
        )
        for k in range(4)
    ]
    distance = rows[0]
    inverse = 1.0 / jnp.sqrt(rows[1] * rows[1] + rows[2] * rows[2] + rows[3] * rows[3])
    normals = [row * inverse for row in rows[1:]]
    geometry_ref[0:1, :] = distance
    for k in range(3):
        geometry_ref[k + 1 : k + 2, :] = normals[k]
    samples = [samples_ref[c : c + 1, :] for c in range(3)]
    stress, _ = wall_solve(samples, distance, normals)
    live = live_row(count_ref, points)
    stress = [jnp.where(live, value, 0.0) for value in stress]
    force = scatter_sum(stress, as_row(wall_ref[...]), live, base_ref.shape)
    for c in range(comps):
        block = force[:, c * nz : (c + 1) * nz] * (TIME_STEP / WALL_DY)
        first_ref[c] = base_ref[c] + block.reshape(nx, ny, nz)
    faces_of(first_ref, xa_ref, xb_ref, ya_ref, yb_ref)


def second_kernel(
    count_ref, rows_ref, turns_ref, velocity_ref, first_ref, wall_ref, geometry_ref,
    part_ref, log_ref, tiles,
):
    comps, nx, ny, nz = first_ref.shape
    points = rows_ref.shape[0]
    samples = sample_at(first_ref, rows_ref, turns_ref, tiles)
    distance = geometry_ref[0:1, :]
    normals = [geometry_ref[k : k + 1, :] for k in range(1, 4)]
    stress, log_stress = wall_solve(samples, distance, normals)
    live = live_row(count_ref, points)
    log_stress = jnp.where(live, log_stress, 0.0)
    for i in range(log_ref.shape[0]):
        log_ref[i : i + 1, :] = log_stress[:, i * 128 : (i + 1) * 128]
    stress = [jnp.where(live, value, 0.0) for value in stress]
    force = scatter_sum(stress, as_row(wall_ref[...]), live, first_ref.shape)
    for c in range(comps):
        block = force[:, c * nz : (c + 1) * nz] * (0.5 * TIME_STEP / WALL_DY)
        part_ref[c] = 0.5 * velocity_ref[c] + block.reshape(nx, ny, nz)


def last_kernel(
    viscosity_ref, first_ref, part_ref, xa_ref, xb_ref, ya_ref, yb_ref,
    advanced_ref, padded, result, sems,
):
    fill_padded(padded, first_ref, xa_ref, xb_ref, ya_ref, yb_ref)

    def emit(spot, value):
        result[spot] = value + part_ref[spot]

    def copy_of(x):
        return pltpu.make_async_copy(
            result.at[:, pl.ds(x, 1)], advanced_ref.at[:, pl.ds(x, 1)], sems.at[x]
        )

    def finish(x):
        copy_of(x).start()

    stencil(padded, viscosity_ref, 0.5 * TIME_STEP, 0.5, emit, finish)

    def settle(x, carry):
        copy_of(x).wait()
        return carry

    lax.fori_loop(0, result.shape[1], settle, 0)


def exchange(faces):
    regions, blocks = lax.axis_size("region"), lax.axis_size("blk")

    def swap(block, partner):
        pairs = []
        for r in range(regions):
            for b in range(blocks):
                to_r, to_b = partner(r, b)
                pairs.append((r * blocks + b, to_r * blocks + to_b))
        return lax.ppermute(block, ("region", "blk"), pairs)

    def x_far(r, b):
        return (r, b ^ 1) if r in (0, regions - 1) else (((r - 1) ^ 1) + 1, b)

    def y_far(r, b):
        return (r ^ 1, b) if b in (0, blocks - 1) else (r, ((b - 1) ^ 1) + 1)

    xa, xb, ya, yb = faces
    return (
        swap(xa, lambda r, b: (r ^ 1, b)),
        swap(xb, x_far),
        swap(ya, lambda r, b: (r, b ^ 1)),
        swap(yb, y_far),
    )


def local(velocity, viscosity, match_cell, wall_cell, match_dest, match_count, wall_geom):
    devices = lax.axis_size("region") * lax.axis_size("blk")
    assert 4 * (wall_geom.shape[1] // devices) == FIELD_LANES
    points = match_cell.shape[0]
    comps, nx, ny, nz = velocity.shape
    field = jax.ShapeDtypeStruct(velocity.shape, F32)
    xface = jax.ShapeDtypeStruct((comps, 2, ny, nz), F32)
    yface = jax.ShapeDtypeStruct((comps, nx, 2, nz), F32)
    rowed = jax.ShapeDtypeStruct((4, points), F32)
    square = (points // 128, 128)
    match = match_cell.reshape(square)
    wall = wall_cell.reshape(square)
    dest = match_dest.reshape(square)
    vmem = pl.BlockSpec(memory_space=pltpu.VMEM)
    limit = pltpu.CompilerParams(vmem_limit_bytes=24 * 1024 * 1024)
    smem = pl.BlockSpec(memory_space=pltpu.SMEM)
    padded = pltpu.VMEM((comps, nz // 128, nx + 4, ny + 16, 128), F32)
    tiles = pltpu.VMEM((TILE_ROWS * nx * ny * (nz // 128) + 8, 128), F32)

    spots = jax.ShapeDtypeStruct(square, jnp.int32)
    outgoing = pl.pallas_call(
        pack_kernel,
        out_shape=jax.ShapeDtypeStruct((devices, 128), F32),
        in_specs=[vmem],
        out_specs=vmem,
        compiler_params=limit,
        cost_estimate=pl.CostEstimate(flops=PACK_COST, bytes_accessed=98304, transcendentals=0),
        name="pack",
    )(pltpu.with_memory_space_constraint(wall_geom, pltpu.HBM))
    arrived = lax.all_to_all(
        outgoing.reshape(devices, 1, 128),
        ("region", "blk"), split_axis=0, concat_axis=0, tiled=True,
    ).reshape(devices, 128)
    *faces, rows, turns = pl.pallas_call(
        faces_kernel,
        out_shape=(xface, xface, yface, yface, spots, spots),
        in_specs=[vmem] * 2,
        out_specs=(vmem,) * 6,
        compiler_params=limit,
        name="faces",
    )(velocity, match)
    rows, turns = rows.reshape(points), turns.reshape(points)
    halos = exchange(faces)
    samples, rank = pl.pallas_call(
        sample_kernel,
        out_shape=(rowed, jax.ShapeDtypeStruct((1, points), F32)),
        in_specs=[smem] * 2 + [vmem] * 2,
        out_specs=(vmem,) * 2,
        scratch_shapes=[tiles],
        compiler_params=limit,
        name="sample",
    )(rows, turns, velocity, dest)
    base = pl.pallas_call(
        rate_kernel,
        out_shape=field,
        in_specs=[vmem] * 6,
        out_specs=vmem,
        scratch_shapes=[padded],
        compiler_params=limit,
        name="rate",
    )(velocity, viscosity, *halos)
    first, *faces, geometry = pl.pallas_call(
        stress_kernel,
        out_shape=(field, xface, xface, yface, yface, rowed),
        in_specs=[smem] + [vmem] * 6,
        out_specs=(vmem,) * 6,
        compiler_params=limit,
        name="stress",
    )(match_count, arrived, dest, wall, rank, samples, base)
    halos = exchange(faces)
    part, log_stress = pl.pallas_call(
        second_kernel,
        out_shape=(field, jax.ShapeDtypeStruct(square, F32)),
        in_specs=[smem] * 3 + [vmem] * 4,
        out_specs=(vmem,) * 2,
        scratch_shapes=[tiles],
        compiler_params=limit,
        name="second",
    )(match_count, rows, turns, velocity, first, wall, geometry)
    advanced = pl.pallas_call(
        last_kernel,
        out_shape=field,
        in_specs=[vmem] * 7,
        out_specs=pl.BlockSpec(memory_space=pl.ANY),
        scratch_shapes=[
            padded, pltpu.VMEM(velocity.shape, F32), pltpu.SemaphoreType.DMA((nx,))
        ],
        compiler_params=limit,
        name="last",
    )(viscosity, first, part, *halos)
    return (advanced, log_stress.reshape(points))


def solution(mesh):
    placed = (
        P(None, "region", "blk", None),
        P("region", "blk", None),
        P(("region", "blk")),
        P(("region", "blk")),
        P(("region", "blk"), None),
        P(("region", "blk")),
        P(None, ("region", "blk")),
    )
    return jax.shard_map(
        local,
        mesh=mesh,
        in_specs=placed,
        out_specs=(P(None, "region", "blk", None), P(("region", "blk"))),
        check_vma=False,
    )
```

```python
import math

import jax
import jax.numpy as jnp
from jax import lax
from jax.experimental import pallas as pl
from jax.experimental.pallas import tpu as pltpu
from jax.sharding import PartitionSpec as P

NEWTON = 2

KAPPA = 0.41
DAMPING = 26.0
NU_WALL = 0.0002
WALL_DY = 0.0005
TIME_STEP = 0.1
SPEED_FLOOR = 0.5
GUESS_RATIO = 14.0
ETAS = 32
PIECES = 2
UNROLL = 4
TILE_ROWS = 3
PACK_COST = 4_000_000_000
FIELD_LANES = 64
F32 = jnp.float32
BF16 = jnp.bfloat16


def pieces_of(values, count):
    parts = []
    rest = values
    for index in range(count):
        part = rest.astype(BF16)
        parts.append(part)
        if index + 1 < count:
            rest = rest - part.astype(F32)
    return parts


def as_row(block):
    rows = block.shape[0]
    return jnp.concatenate([block[i : i + 1, :] for i in range(rows)], axis=1)


def row_iota(shape):
    return lax.broadcasted_iota(jnp.int32, shape, 0)


def even_side(axis):
    return lax.axis_index(axis) % 2 == 0


def at_end(axis):
    place = lax.axis_index(axis)
    return (place == 0) | (place == lax.axis_size(axis) - 1)


def fill_padded(padded, field_ref, xa_ref, xb_ref, ya_ref, yb_ref):
    comps, nx, ny, nz = field_ref.shape
    even_x, even_y = even_side("region"), even_side("blk")
    end_x, end_y = at_end("region"), at_end("blk")
    spot_a = jnp.where(even_x, nx + 2, 0)
    spot_b = nx + 2 - spot_a
    for c in range(comps):
        near_x = xa_ref[c]
        far_x = jnp.where(end_x, 0.0, xb_ref[c])
        near_y = ya_ref[c]
        far_y = jnp.where(end_y, 0.0, yb_ref[c])
        low_y = jnp.where(even_y, far_y, near_y)
        high_y = jnp.where(even_y, near_y, far_y)
        for h in range(nz // 128):
            lanes = slice(128 * h, 128 * h + 128)
            padded[c, h, 2 : 2 + nx, 8 : 8 + ny, :] = field_ref[c, :, :, lanes]
            padded[c, h, pl.ds(spot_a, 2), 8 : 8 + ny, :] = near_x[:, :, lanes]
            padded[c, h, pl.ds(spot_b, 2), 8 : 8 + ny, :] = far_x[:, :, lanes]
            padded[c, h, 2 : 2 + nx, 6:8, :] = low_y[:, :, lanes]
            padded[c, h, 2 : 2 + nx, 8 + ny : 10 + ny, :] = high_y[:, :, lanes]


def stencil(padded, viscosity_ref, step, keep, emit, finish=None):
    comps, halves = padded.shape[:2]
    nx, ny, _ = viscosity_ref.shape
    lane = lax.broadcasted_iota(jnp.int32, (8, 128), 1)
    top = [lane < 127, lane < 126]
    bottom = [lane >= 1, lane >= 2]
    scale = step / 12.0

    def plane(x, carry):
        for tile in range(ny // 8):
            y = 8 + 8 * tile
            here = [
                [padded[c, h, x + 2, y : y + 8, :] for h in range(halves)] for c in range(comps)
            ]
            for h in range(halves):
                lanes = slice(128 * h, 128 * h + 128)
                visc = viscosity_ref[x, 8 * tile : 8 * tile + 8, lanes] * scale
                visc_near = 16.0 * visc
                center = keep - 90.0 * visc
                speed = [here[c][h] * scale for c in range(comps)]
                for c in range(comps):

                    def along_z(shift):
                        count = abs(shift)
                        rolled = pltpu.roll(here[c][h], (-shift) % 128, 1)
                        other = h + (1 if shift > 0 else -1)
                        if 0 <= other < halves:
                            rest = pltpu.roll(here[c][other], (-shift) % 128, 1)
                        else:
                            rest = 0.0
                        inside = top[count - 1] if shift > 0 else bottom[count - 1]
                        return jnp.where(inside, rolled, rest)

                    def at(axis, shift):
                        if axis == 0:
                            return padded[c, h, x + 2 + shift, y : y + 8, :]
                        if axis == 1:
                            return padded[c, h, x + 2, y + shift : y + shift + 8, :]
                        return along_z(shift)

                    for axis in range(3):
                        a1, b1, a2, b2 = (at(axis, shift) for shift in (1, -1, 2, -2))
                        slope = 8.0 * (a1 - b1) - (a2 - b2)
                        if axis == 0:
                            near, far = a1 + b1, a2 + b2
                            advect = speed[axis] * slope
                        else:
                            near, far = near + (a1 + b1), far + (a2 + b2)
                            advect = advect + speed[axis] * slope
                    rows = slice(8 * tile, 8 * tile + 8)
                    value = center * here[c][h] + visc_near * near - visc * far - advect
                    emit((c, x, rows, lanes), value)
        if finish is not None:
            finish(x)
        return carry

    lax.fori_loop(0, nx, plane, 0, unroll=UNROLL)


def lay_tiles(field_ref, tiles):
    comps, nx, ny, nz = field_ref.shape
    for c in range(comps):
        for x in range(nx):
            for y in range(0, ny, 8):
                for h in range(nz // 128):
                    start = ((h * nx + x) * ny + y) * TILE_ROWS + c
                    tiles[pl.ds(start, 8, stride=TILE_ROWS), :] = field_ref[
                        c, x, y : y + 8, 128 * h : 128 * h + 128
                    ]


def sample_at(tiles, comps, rows_ref, turns_ref):
    lane = lax.broadcasted_iota(jnp.int32, (8, 128), 1)
    blocks = []
    for start in range(0, rows_ref.shape[0], 128):
        parts = []
        for low in range(0, 128, 32):
            part = jnp.zeros((8, 128), F32)
            for spot in range(low, low + 32):
                row = rows_ref[start + spot]
                turned = pltpu.roll(tiles[pl.ds(row, 8), :], turns_ref[start + spot], 1)
                part = jnp.where(lane == spot, turned, part)
            parts.append(part)
        blocks.append((parts[0] + parts[1]) + (parts[2] + parts[3]))
    return [jnp.concatenate([block[c : c + 1] for block in blocks], axis=1) for c in range(comps)]


def scatter_sum(stresses, cells, live, shape):
    comps, nx, ny, nz = shape
    points = cells.shape[1]
    rows = nx * ny
    lane_cell = cells & (nz - 1)
    row_cell = cells // nz
    hot = jnp.where(row_iota((rows, points)) == row_cell, 1.0, 0.0).astype(BF16)
    match = (row_iota((nz, points)) == lane_cell) & live
    total = None
    split = [pieces_of(value, PIECES) for value in stresses]
    for index in range(PIECES):
        spread = jnp.concatenate(
            [
                jnp.where(match, split[c][index].astype(F32), 0.0).astype(BF16)
                for c in range(comps)
            ],
            axis=0,
        )
        part = lax.dot_general(
            hot, spread, (((1,), (1,)), ((), ())), preferred_element_type=F32
        )
        total = part if total is None else total + part
    return total


def wall_solve(samples, distance, normals):
    points = distance.shape[1]
    normal_part = sum(s * n for s, n in zip(samples, normals))
    tangent = [s - normal_part * n for s, n in zip(samples, normals)]
    speed = jnp.maximum(jnp.sqrt(sum(t * t for t in tangent)), SPEED_FLOOR)
    target = jnp.log(speed)
    log_speed = target - math.log(GUESS_RATIO)
    index = row_iota((ETAS, points)).astype(F32)
    top = ETAS - 1.0
    eta = (index / top) * (index / top)
    upper = jnp.minimum(index + 1.0, top) / top
    lower = jnp.maximum(index - 1.0, 0.0) / top
    weight = 0.5 * (upper * upper - lower * lower)
    for _ in range(NEWTON):
        pace = jnp.exp(log_speed)
        height = eta * (distance * pace)
        decay = height * (1.0 / (NU_WALL * DAMPING))
        fade = jnp.exp(-decay)
        damp = 1.0 - fade
        mixing = KAPPA * height * damp
        inverse = 1.0 / (NU_WALL + mixing * damp)
        growth = mixing * (damp + 2.0 * decay * fade)
        share = weight * inverse
        total = jnp.sum(share, axis=0, keepdims=True)
        change = jnp.sum(share * (growth * inverse), axis=0, keepdims=True)
        value = jnp.log(distance * pace * pace * total) - target
        log_speed = log_speed - value / (2.0 - change / total)
    stress = jnp.exp(2.0 * log_speed)
    factor = -stress / speed
    return [factor * t for t in tangent], 2.0 * log_speed


def sample_kernel(rows_ref, turns_ref, velocity_ref, dest_ref, samples_ref, rank_ref, tiles):
    points = rows_ref.shape[0]
    lay_tiles(velocity_ref, tiles)
    samples = sample_at(tiles, velocity_ref.shape[0], rows_ref, turns_ref)
    for c in range(3):
        samples_ref[c : c + 1, :] = samples[c]
    owners = as_row(dest_ref[...])
    devices = lax.axis_size("region") * lax.axis_size("blk")
    width = 128
    before = jnp.where(
        row_iota((width, width)) < lax.broadcasted_iota(jnp.int32, (width, width), 1), 1.0, 0.0
    )
    table = jnp.concatenate([before, jnp.ones((width, width), F32)], axis=0).astype(BF16)
    earlier = jnp.zeros((devices, width), F32)
    for start in range(0, points, width):
        hot = jnp.where(row_iota((devices, width)) == owners[:, start : start + width], 1.0, 0.0)
        both = jnp.concatenate([hot, earlier], axis=1).astype(BF16)
        running = jnp.dot(both, table, preferred_element_type=F32)
        rank_ref[0:1, start : start + width] = jnp.sum(hot * running, axis=0, keepdims=True)
        earlier = earlier + hot


def rate_kernel(
    velocity_ref, viscosity_ref, xa_ref, xb_ref, ya_ref, yb_ref, base_ref, padded
):
    fill_padded(padded, velocity_ref, xa_ref, xb_ref, ya_ref, yb_ref)

    def emit(spot, value):
        base_ref[spot] = value

    stencil(padded, viscosity_ref, TIME_STEP, 1.0, emit)


def pair_spot(nx):
    return jnp.where(even_side("region"), nx - 2, 0)


def faces_kernel(
    velocity_ref, match_ref, xa_ref, xb_ref, ya_ref, yb_ref, rows_ref, turns_ref
):
    _, nx, ny, nz = velocity_ref.shape
    cells = match_ref[...]
    half, row = (cells // 128) % (nz // 128), cells // nz
    rows_ref[...] = (half * (nx * ny) + row) * TILE_ROWS
    turns_ref[...] = (lax.broadcasted_iota(jnp.int32, cells.shape, 1) - cells) & 127
    faces_of(velocity_ref, xa_ref, xb_ref, ya_ref, yb_ref)


def faces_of(field_ref, xa_ref, xb_ref, ya_ref, yb_ref):
    comps, nx, ny, _ = field_ref.shape
    spot = pair_spot(nx)
    even_y = even_side("blk")
    for c in range(comps):
        xa_ref[c] = field_ref[c, pl.ds(spot, 2)]
        xb_ref[c] = field_ref[c, pl.ds(nx - 2 - spot, 2)]
        low, high = field_ref[c, :, 0:2, :], field_ref[c, :, ny - 2 : ny, :]
        ya_ref[c] = jnp.where(even_y, high, low)
        yb_ref[c] = jnp.where(even_y, low, high)


def pack_kernel(geometry_ref, out_ref):
    fields, faces = geometry_ref.shape
    devices = out_ref.shape[0]
    capacity = faces // devices
    lane = lax.broadcasted_iota(jnp.int32, (8, 128), 1)
    for tile in range(devices // 8):
        rows = None
        for k in range(fields):
            line = geometry_ref[k : k + 1, 128 * tile : 128 * tile + 128]
            wide = jnp.broadcast_to(line, (8, 128))
            moved = pltpu.roll(wide, capacity, 1, stride=capacity, stride_axis=0)
            if k > 0:
                moved = pltpu.roll(moved, k * capacity, 1)
            rows = moved if rows is None else jnp.where(lane >= k * capacity, moved, rows)
        for i in range(8):
            out_ref[8 * tile + 7 - i : 8 * tile + 8 - i, :] = rows[i : i + 1, :]


def live_row(count_ref, points):
    return lax.broadcasted_iota(jnp.int32, (1, points), 1) < count_ref[0]


def stress_kernel(
    count_ref, arrived_ref, dest_ref, wall_ref, rank_ref, samples_ref, base_ref,
    first_ref, xa_ref, xb_ref, ya_ref, yb_ref, geometry_ref, tiles,
):
    comps, nx, ny, nz = base_ref.shape
    devices = arrived_ref.shape[0]
    capacity = FIELD_LANES // 4
    points = wall_ref.shape[0] * wall_ref.shape[1]
    owners = as_row(dest_ref[...])
    hot = jnp.where(row_iota((devices, points)) == owners, 1.0, 0.0).astype(BF16)
    table = None
    for part in pieces_of(arrived_ref[:, :FIELD_LANES], 3):
        term = lax.dot_general(
            part, hot, (((0,), (0,)), ((), ())), preferred_element_type=F32
        )
        table = term if table is None else table + term
    rank = rank_ref[0:1, :].astype(jnp.int32)
    mask = row_iota((capacity, points)) == rank
    rows = [
        jnp.sum(
            jnp.where(mask, table[k * capacity : (k + 1) * capacity, :], 0.0),
            axis=0, keepdims=True,
        )
        for k in range(4)
    ]
    distance = rows[0]
    inverse = 1.0 / jnp.sqrt(rows[1] * rows[1] + rows[2] * rows[2] + rows[3] * rows[3])
    normals = [row * inverse for row in rows[1:]]
    geometry_ref[0:1, :] = distance
    for k in range(3):
        geometry_ref[k + 1 : k + 2, :] = normals[k]
    samples = [samples_ref[c : c + 1, :] for c in range(3)]
    stress, _ = wall_solve(samples, distance, normals)
    live = live_row(count_ref, points)
    stress = [jnp.where(live, value, 0.0) for value in stress]
    force = scatter_sum(stress, as_row(wall_ref[...]), live, base_ref.shape)
    for c in range(comps):
        block = force[:, c * nz : (c + 1) * nz] * (TIME_STEP / WALL_DY)
        first_ref[c] = base_ref[c] + block.reshape(nx, ny, nz)
    faces_of(first_ref, xa_ref, xb_ref, ya_ref, yb_ref)
    lay_tiles(first_ref, tiles)


def second_kernel(
    count_ref, rows_ref, turns_ref, velocity_ref, tiles, wall_ref, geometry_ref,
    part_ref, log_ref,
):
    comps, nx, ny, nz = velocity_ref.shape
    points = rows_ref.shape[0]
    samples = sample_at(tiles, comps, rows_ref, turns_ref)
    distance = geometry_ref[0:1, :]
    normals = [geometry_ref[k : k + 1, :] for k in range(1, 4)]
    stress, log_stress = wall_solve(samples, distance, normals)
    live = live_row(count_ref, points)
    log_stress = jnp.where(live, log_stress, 0.0)
    for i in range(log_ref.shape[0]):
        log_ref[i : i + 1, :] = log_stress[:, i * 128 : (i + 1) * 128]
    stress = [jnp.where(live, value, 0.0) for value in stress]
    force = scatter_sum(stress, as_row(wall_ref[...]), live, velocity_ref.shape)
    for c in range(comps):
        block = force[:, c * nz : (c + 1) * nz] * (0.5 * TIME_STEP / WALL_DY)
        part_ref[c] = 0.5 * velocity_ref[c] + block.reshape(nx, ny, nz)


def last_kernel(
    viscosity_ref, first_ref, part_ref, xa_ref, xb_ref, ya_ref, yb_ref,
    advanced_ref, padded, result, sems,
):
    fill_padded(padded, first_ref, xa_ref, xb_ref, ya_ref, yb_ref)

    def emit(spot, value):
        result[spot] = value + part_ref[spot]

    def copy_of(x):
        return pltpu.make_async_copy(
            result.at[:, pl.ds(x, 1)], advanced_ref.at[:, pl.ds(x, 1)], sems.at[x]
        )

    def finish(x):
        copy_of(x).start()

    stencil(padded, viscosity_ref, 0.5 * TIME_STEP, 0.5, emit, finish)

    def settle(x, carry):
        copy_of(x).wait()
        return carry

    lax.fori_loop(0, result.shape[1], settle, 0)


def exchange(faces):
    regions, blocks = lax.axis_size("region"), lax.axis_size("blk")

    def swap(block, partner):
        pairs = []
        for r in range(regions):
            for b in range(blocks):
                to_r, to_b = partner(r, b)
                pairs.append((r * blocks + b, to_r * blocks + to_b))
        return lax.ppermute(block, ("region", "blk"), pairs)

    def x_far(r, b):
        return (r, b ^ 1) if r in (0, regions - 1) else (((r - 1) ^ 1) + 1, b)

    def y_far(r, b):
        return (r ^ 1, b) if b in (0, blocks - 1) else (r, ((b - 1) ^ 1) + 1)

    xa, xb, ya, yb = faces
    return (
        swap(xa, lambda r, b: (r ^ 1, b)),
        swap(xb, x_far),
        swap(ya, lambda r, b: (r, b ^ 1)),
        swap(yb, y_far),
    )


def local(velocity, viscosity, match_cell, wall_cell, match_dest, match_count, wall_geom):
    devices = lax.axis_size("region") * lax.axis_size("blk")
    assert 4 * (wall_geom.shape[1] // devices) == FIELD_LANES
    points = match_cell.shape[0]
    comps, nx, ny, nz = velocity.shape
    field = jax.ShapeDtypeStruct(velocity.shape, F32)
    xface = jax.ShapeDtypeStruct((comps, 2, ny, nz), F32)
    yface = jax.ShapeDtypeStruct((comps, nx, 2, nz), F32)
    rowed = jax.ShapeDtypeStruct((4, points), F32)
    square = (points // 128, 128)
    match = match_cell.reshape(square)
    wall = wall_cell.reshape(square)
    dest = match_dest.reshape(square)
    vmem = pl.BlockSpec(memory_space=pltpu.VMEM)
    limit = pltpu.CompilerParams(vmem_limit_bytes=24 * 1024 * 1024)
    smem = pl.BlockSpec(memory_space=pltpu.SMEM)
    padded = pltpu.VMEM((comps, nz // 128, nx + 4, ny + 16, 128), F32)
    tiles = pltpu.VMEM((TILE_ROWS * nx * ny * (nz // 128) + 8, 128), F32)

    spots = jax.ShapeDtypeStruct(square, jnp.int32)
    outgoing = pl.pallas_call(
        pack_kernel,
        out_shape=jax.ShapeDtypeStruct((devices, 128), F32),
        in_specs=[vmem],
        out_specs=vmem,
        compiler_params=limit,
        cost_estimate=pl.CostEstimate(flops=PACK_COST, bytes_accessed=98304, transcendentals=0),
        name="pack",
    )(pltpu.with_memory_space_constraint(wall_geom, pltpu.HBM))
    arrived = lax.all_to_all(
        outgoing.reshape(devices, 1, 128),
        ("region", "blk"), split_axis=0, concat_axis=0, tiled=True,
    ).reshape(devices, 128)
    *faces, rows, turns = pl.pallas_call(
        faces_kernel,
        out_shape=(xface, xface, yface, yface, spots, spots),
        in_specs=[vmem] * 2,
        out_specs=(vmem,) * 6,
        compiler_params=limit,
        name="faces",
    )(velocity, match)
    rows, turns = rows.reshape(points), turns.reshape(points)
    halos = exchange(faces)
    samples, rank = pl.pallas_call(
        sample_kernel,
        out_shape=(rowed, jax.ShapeDtypeStruct((1, points), F32)),
        in_specs=[smem] * 2 + [vmem] * 2,
        out_specs=(vmem,) * 2,
        scratch_shapes=[tiles],
        compiler_params=limit,
        name="sample",
    )(rows, turns, velocity, dest)
    base = pl.pallas_call(
        rate_kernel,
        out_shape=field,
        in_specs=[vmem] * 6,
        out_specs=vmem,
        scratch_shapes=[padded],
        compiler_params=limit,
        name="rate",
    )(velocity, viscosity, *halos)
    first, *faces, geometry, laid = pl.pallas_call(
        stress_kernel,
        out_shape=(
            field, xface, xface, yface, yface, rowed,
            jax.ShapeDtypeStruct(tiles.shape, F32),
        ),
        in_specs=[smem] + [vmem] * 6,
        out_specs=(vmem,) * 7,
        compiler_params=limit,
        name="stress",
    )(match_count, arrived, dest, wall, rank, samples, base)
    halos = exchange(faces)
    part, log_stress = pl.pallas_call(
        second_kernel,
        out_shape=(field, jax.ShapeDtypeStruct(square, F32)),
        in_specs=[smem] * 3 + [vmem] * 4,
        out_specs=(vmem,) * 2,
        compiler_params=limit,
        name="second",
    )(match_count, rows, turns, velocity, laid, wall, geometry)
    advanced = pl.pallas_call(
        last_kernel,
        out_shape=field,
        in_specs=[vmem] * 7,
        out_specs=pl.BlockSpec(memory_space=pl.ANY),
        scratch_shapes=[
            padded, pltpu.VMEM(velocity.shape, F32), pltpu.SemaphoreType.DMA((nx,))
        ],
        compiler_params=limit,
        name="last",
    )(viscosity, first, part, *halos)
    return (advanced, log_stress.reshape(points))


def solution(mesh):
    placed = (
        P(None, "region", "blk", None),
        P("region", "blk", None),
        P(("region", "blk")),
        P(("region", "blk")),
        P(("region", "blk"), None),
        P(("region", "blk")),
        P(None, ("region", "blk")),
    )
    return jax.shard_map(
        local,
        mesh=mesh,
        in_specs=placed,
        out_specs=(P(None, "region", "blk", None), P(("region", "blk"))),
        check_vma=False,
    )
```
